256 devices in a mesh: lat: 32 (over z, x), lev: 8 (over y, core).
Axes of the slice: x: 4, y: 4, z: 8, core: 2. Of those that a mesh axis runs over, the one named last changes fastest.
Arguments:
- tokens: bfloat16 [2, 8, 64, 64, 1024], P(None, 'lev', 'lat'), may hold values from -40 to 40
- key_mask: int32 [2, 64], replicated, may hold values from 0 to 1, as said below
- w_qkv: bfloat16 [1024, 3072], replicated, may hold values from -0.1875 to 0.1875
- w_mix: bfloat16 [8, 1024, 1024], P('lev'), may hold values from -0.0625 to 0.0625
- level_scale: float32 [8, 1024], P('lev'), may hold values from 0.1 to 1.9
- cotangent: bfloat16 [2, 8, 64, 64, 1024], P(None, 'lev', 'lat'), may hold values from -6 to 6
Outputs:
- output: bfloat16 [2, 8, 64, 64, 1024], P(None, 'lev', 'lat')
- d_tokens: bfloat16 [2, 8, 64, 64, 1024], P(None, 'lev', 'lat')
- mix_grad: float32 [8, 1024, 1024], P('lev', 'lat')
The draws below stay inside these ranges and needn't reach their ends.
Inputs may be any that keep to these rules, and one draw needn't show every extreme that they name: `key_mask`: each sample has 1 to 4 padded rows, all at the end of the latitude rows, and the rest real; some sample has exactly 4 padded rows.
All inputs are finite; a program needn't handle non-finite values.
Results may differ from the reference program's by a relative error of at most 0.015.
Values may be sent and summed in bfloat16 or wider, within the bound.
A program may use at most 128 MiB of HBM per device.

```python
import math
import jax
import jax.numpy as jnp
from jax import lax

WIDTH = 1024
HEADS = 16
HEAD_DIM = 64
LON = 64
LAT = 64
LEV = 8
BATCH = 2
PAD_MOST = 4


def draw_tokens(key, part):
    base_key, row_key, col_key = jax.random.split(key, 3)
    full_shape = (BATCH, LEV, LAT, LON, WIDTH)
    log_low = math.log(0.3)
    log_high = math.log(3.0)
    row_scale = jnp.exp(jax.random.uniform(row_key, full_shape[:-1] + (1,), jnp.float32, log_low, log_high))
    col_scale = jnp.exp(jax.random.uniform(col_key, (WIDTH,), jnp.float32, log_low, log_high))
    base_values = jnp.clip(jax.random.normal(base_key, full_shape, jnp.float32), -4.0, 4.0)
    return (base_values * row_scale * col_scale).astype(jnp.bfloat16)


def draw_key_mask(key, part):
    count_key, pick_key = jax.random.split(key)
    pad_rows = jax.random.randint(count_key, (BATCH,), 1, PAD_MOST + 1).astype(jnp.int32)
    chosen = jax.random.randint(pick_key, (), 0, BATCH).astype(jnp.int32)
    sample_index = jnp.arange(BATCH, dtype=jnp.int32)
    pad_rows = jnp.where(sample_index == chosen, jnp.int32(PAD_MOST), pad_rows).astype(jnp.int32)
    lat_index = jnp.arange(LAT, dtype=jnp.int32)
    return (lat_index[None, :] < (LAT - pad_rows)[:, None]).astype(jnp.int32)


def block_levels(rng, shape, cuts, least, largest):
    def one(axis_at, parts):
        draws = jax.random.uniform(jax.random.fold_in(jax.random.fold_in(rng, 6), axis_at), (parts,), jnp.float32, least / len(cuts), largest / len(cuts))
        return jnp.repeat(jnp.exp(draws), shape[axis_at] // parts).reshape((-1,) + (1,) * (len(shape) - axis_at - 1))

    level = one(*cuts[0])
    for cut in cuts[1:]:
        level = level * one(*cut)
    return level


def noise(key, shape, deviation, reach, cuts=(), held_as=jnp.bfloat16):
    values = deviation * jax.random.normal(key, shape, jnp.float32)
    if cuts:
        values = values * block_levels(key, shape, cuts, -0.22, 0.18)
    return jnp.clip(values, -reach, reach).astype(held_as)


def setup_inputs(seed: int = 0) -> dict:
    seeds = jax.random.split(jax.random.key(seed), 7)
    tokens = draw_tokens(jax.random.fold_in(seeds[6], 71), 0)
    key_mask = draw_key_mask(jax.random.fold_in(seeds[6], 71), 0)
    w_qkv = noise(seeds[2], (WIDTH, 3 * WIDTH), WIDTH ** -0.5, 0.1875)
    w_mix = noise(seeds[3], (LEV, WIDTH, WIDTH), (WIDTH * LEV) ** -0.5, 0.0625, ((0, 8),))
    level_scale = jnp.clip(1.0 + 0.18 * jax.random.normal(seeds[4], (LEV, WIDTH), jnp.float32), 0.1, 1.9)
    cotangent = noise(seeds[5], (BATCH, LEV, LAT, LON, WIDTH), 1.0, 6.0, ((1, 8), (2, 32)))
    return dict(tokens=tokens, key_mask=key_mask, w_qkv=w_qkv, w_mix=w_mix, level_scale=level_scale, cotangent=cotangent)


epsilon = 1e-06
score_scale = 0.25

def rms_factor(values):
    return lax.rsqrt(lax.optimization_barrier(jnp.mean(values * values, axis=-1, keepdims=True)) + epsilon)

def norm_backward(values, factor, upstream):
    inner_mean = lax.optimization_barrier(jnp.mean(upstream * values, axis=-1, keepdims=True))
    return factor * upstream - values * (factor * factor * factor) * inner_mean

def attention_weights(query_heads, key_heads, valid_keys):
    scores = jnp.einsum('bijne,bkjne->bjnik', query_heads.astype(jnp.float32), key_heads.astype(jnp.float32)) * score_scale
    exp_scores = jnp.exp(scores) * valid_keys.astype(jnp.float32)[:, None, None, None, :]
    return exp_scores / lax.optimization_barrier(jnp.sum(exp_scores, axis=-1, keepdims=True))

def project(level_tokens, w_qkv):
    tokens_f32 = level_tokens.astype(jnp.float32)
    factor = rms_factor(tokens_f32)
    normed = (tokens_f32 * factor).astype(jnp.bfloat16)
    projected = jnp.dot(normed.reshape(-1, WIDTH), w_qkv, preferred_element_type=jnp.float32)
    head_shape = level_tokens.shape[:-1] + (HEADS, HEAD_DIM)
    query = projected[:, :WIDTH].reshape(head_shape)
    key_raw = projected[:, WIDTH:2 * WIDTH].reshape(head_shape)
    value = projected[:, 2 * WIDTH:].reshape(head_shape)
    query_factor = rms_factor(query)
    key_factor = rms_factor(key_raw)
    query_norm = (query * query_factor).astype(jnp.bfloat16)
    key_norm = (key_raw * key_factor).astype(jnp.bfloat16)
    value_cast = value.astype(jnp.bfloat16)
    return (tokens_f32, factor, normed, query, query_factor, key_raw, key_factor, query_norm, key_norm, value_cast)

def reference(tokens, key_mask, w_qkv, w_mix, level_scale, cotangent):
    by_level = jnp.moveaxis(tokens, 1, 0)
    cot_by_level = jnp.moveaxis(cotangent, 1, 0)

    def forward_level(mix_total, inputs):
        level_tokens, mixer_level = inputs
        pieces = project(level_tokens, w_qkv)
        weights = attention_weights(pieces[7], pieces[8], key_mask)
        weights_b = lax.optimization_barrier(weights.astype(jnp.bfloat16)).astype(jnp.float32)
        attended = jnp.einsum('bjnik,bkjne->bijne', weights_b, pieces[9].astype(jnp.float32)).astype(jnp.bfloat16)
        attended = attended.reshape(level_tokens.shape)
        mix_total = mix_total + jnp.dot(attended.reshape(-1, WIDTH), mixer_level, preferred_element_type=jnp.float32)
        return (mix_total, attended)
    zero_total = jnp.zeros((BATCH * LAT * LON, WIDTH), jnp.float32)
    mix_total, attended_all = lax.scan(forward_level, zero_total, (by_level, w_mix))
    level_mix = mix_total.reshape(BATCH, 1, LAT, LON, WIDTH)
    level_gain = level_scale[None, :, None, None, :]
    output = (tokens.astype(jnp.float32) + level_gain * level_mix).astype(jnp.bfloat16)
    flow_total = lax.optimization_barrier(jnp.sum(level_gain * cotangent.astype(jnp.float32), axis=1))
    flow_b = flow_total.astype(jnp.bfloat16).reshape(-1, WIDTH)
    token_total = BATCH * LAT * LON

    def backward_level(unused_carry, inputs):
        level_tokens, mixer_level, attended, level_cotangent = inputs
        grad_mix = jnp.dot(attended.reshape(-1, WIDTH).T, flow_b, preferred_element_type=jnp.float32) / math.sqrt(token_total)
        head_shape = level_tokens.shape[:-1] + (HEADS, HEAD_DIM)
        d_attended = jnp.dot(flow_b, mixer_level.T, preferred_element_type=jnp.float32).astype(jnp.bfloat16).reshape(head_shape)
        tokens_f32, factor, normed, query, query_factor, key_raw, key_factor, query_norm, key_norm, value_cast = project(level_tokens, w_qkv)
        weights = attention_weights(query_norm, key_norm, key_mask)
        weights_b = lax.optimization_barrier(weights.astype(jnp.bfloat16)).astype(jnp.float32)
        d_float = d_attended.astype(jnp.float32)
        d_value = jnp.einsum('bjnik,bijne->bkjne', weights_b, d_float).astype(jnp.bfloat16)
        d_attn = jnp.einsum('bijne,bkjne->bjnik', d_float, value_cast.astype(jnp.float32))
        d_scores = weights * (d_attn - lax.optimization_barrier(jnp.sum(weights * d_attn, axis=-1, keepdims=True)))
        d_scores_b = lax.optimization_barrier((d_scores * score_scale).astype(jnp.bfloat16)).astype(jnp.float32)
        d_query = jnp.einsum('bjnik,bkjne->bijne', d_scores_b, key_norm.astype(jnp.float32)).astype(jnp.bfloat16)
        d_key = jnp.einsum('bjnik,bijne->bkjne', d_scores_b, query_norm.astype(jnp.float32)).astype(jnp.bfloat16)
        grad_query = norm_backward(query, query_factor, d_query.astype(jnp.float32))
        grad_key = norm_backward(key_raw, key_factor, d_key.astype(jnp.float32))
        grad_proj = jnp.concatenate([grad_query.reshape(-1, WIDTH), grad_key.reshape(-1, WIDTH), d_value.astype(jnp.float32).reshape(-1, WIDTH)], axis=1).astype(jnp.bfloat16)
        d_normed = jnp.dot(grad_proj, w_qkv.T, preferred_element_type=jnp.float32).reshape(level_tokens.shape)
        d_level = (level_cotangent.astype(jnp.float32) + norm_backward(tokens_f32, factor, d_normed)).astype(jnp.bfloat16)
        return (unused_carry, (d_level, grad_mix))
    _, (d_levels, mix_grad) = lax.scan(backward_level, jnp.zeros((), jnp.float32), (by_level, w_mix, attended_all, cot_by_level))
    d_tokens = jnp.moveaxis(d_levels, 0, 1)
    return (output, d_tokens, mix_grad)
```

```python
import functools
import math
from types import SimpleNamespace

import jax
import jax.numpy as jnp
from jax import lax
from jax.experimental import pallas as pl
from jax.experimental.pallas import tpu as pltpu
from jax.sharding import PartitionSpec as P

HEAD = 64
QUAD = 256
X_CHIPS = 4
epsilon = 1e-06
score_scale = 0.25
f32 = jnp.float32
bf16 = jnp.bfloat16
MESH = pl.DeviceIdType.MESH


def dot(a, b):
    return lax.dot_general(a, b, (((1,), (0,)), ((), ())), preferred_element_type=f32)


def dot_nt(a, b):
    return lax.dot_general(a, b, (((1,), (1,)), ((), ())), preferred_element_type=f32)


def dot_tn(a, b):
    return lax.dot_general(a, b, (((0,), (0,)), ((), ())), preferred_element_type=f32)


def log2(n):
    return n.bit_length() - 1


def lat_to_block(d, a):
    j = a >> log2(d.m)
    b = (a >> log2(d.rb * d.pl)) & (d.batch - 1)
    r = (a >> log2(d.pl)) & (d.rb - 1)
    p = a & (d.pl - 1)
    return (b * d.rb + r) * d.lon + j * d.pl + p


def block_to_group(d, c):
    b = c >> log2(d.pl * d.lat)
    p = (c >> log2(d.lat)) & (d.pl - 1)
    i = (c & (d.lat - 1)) >> log2(d.rb)
    r = c & (d.rb - 1)
    return i * d.m + b * d.rb * d.pl + r * d.pl + p


def permutation(d, index, forward):
    rows = lax.broadcasted_iota(jnp.int32, (d.tokens, d.tokens), 0)
    cols = lax.broadcasted_iota(jnp.int32, (d.tokens, d.tokens), 1)
    hit = index(d, rows) == cols if forward else index(d, cols) == rows
    return jnp.where(hit, 1.0, 0.0).astype(bf16)


def group_sum(values, ones):
    high = values.astype(bf16)
    low = (values - high.astype(f32)).astype(bf16)
    return dot(high, ones) + dot(low, ones)


def kernel(
    d,
    tok_hbm,
    mask_ref,
    wq_hbm,
    wm_hbm,
    scale_ref,
    cot_hbm,
    out_ref,
    dtok_ref,
    mg_ref,
    tok_v,
    cot_v,
    wq_v,
    wm_v,
    send_t,
    recv_t,
    send_f,
    recv_f,
    send_fa,
    recv_fa,
    flow_full,
    send_m,
    recv_m,
    send_ma,
    recv_ma,
    mix_full,
    send_d,
    recv_d,
    mg_s,
    recv_g1,
    send_g2,
    recv_g2,
    xg,
    rx_s,
    normed_s,
    raw_s,
    fac_s,
    qkv_s,
    attn_s,
    att_s,
    flow_a,
    flow_g,
    gp_s,
    dn_s,
    maskf,
    load_sem,
    send_sem,
    recv_sem,
):
    me = lax.axis_index("lat")
    lv = lax.axis_index("lev")
    nl, nv, m, width, tokens = d.nl, d.nv, d.m, d.width, d.tokens
    piece = d.piece
    loads = [
        pltpu.make_async_copy(src, dst, load_sem.at[n])
        for n, (src, dst) in enumerate(
            ((tok_hbm, tok_v), (cot_hbm, cot_v), (wq_hbm, wq_v), (wm_hbm, wm_v))
        )
    ]
    for load in loads:
        load.start()

    barrier = pltpu.get_barrier_semaphore()

    def greet_lat(k, carry):
        pl.semaphore_signal(
            barrier, inc=1, device_id={"lat": lax.rem(me + k, nl)}, device_id_type=MESH
        )
        return carry

    def greet_lev(k, carry):
        pl.semaphore_signal(
            barrier, inc=1, device_id={"lev": lax.rem(lv + k, nv)}, device_id_type=MESH
        )
        return carry

    lax.fori_loop(1, nl, greet_lat, 0)
    lax.fori_loop(1, nv, greet_lev, 0)

    def lat_copy(src, dst, sem, peer):
        return pltpu.make_async_remote_copy(
            src_ref=src,
            dst_ref=dst,
            send_sem=send_sem.at[sem],
            recv_sem=recv_sem.at[sem],
            device_id={"lat": peer},
            device_id_type=MESH,
        )

    def lev_copy(src, dst, sem, peer):
        return pltpu.make_async_remote_copy(
            src_ref=src,
            dst_ref=dst,
            send_sem=send_sem.at[sem],
            recv_sem=recv_sem.at[sem],
            device_id={"lev": peer},
            device_id_type=MESH,
        )

    def all_to_all(send, recv, sem):
        def body(k, carry):
            peer = lax.rem(me + k, nl)
            lat_copy(send.at[peer], recv.at[me], sem, peer).start()
            return carry

        lax.fori_loop(1, nl, body, 0)
        recv[me] = send[me]

    def all_to_all_done(send, recv, sem):
        return lat_copy(
            send.at[pl.ds(0, nl - 1)], recv.at[pl.ds(0, nl - 1)], sem, lax.rem(me + 1, nl)
        )

    def lanes(index):
        return pl.ds(pl.multiple_of(index * piece, piece), piece)

    def level_scatter(send, recv, sem):
        def body(k, carry):
            peer = lax.rem(lv + k, nv)
            lev_copy(send.at[:, :, lanes(peer)], recv.at[k - 1], sem, peer).start()
            return carry

        lax.fori_loop(1, nv, body, 0)

    def level_sum(send, recv, sem):
        lev_copy(recv, recv, sem, lax.rem(lv + 1, nv)).wait_recv()
        total = send[:, :, lanes(lv)].astype(f32)
        for k in range(nv - 1):
            total = total + recv[k].astype(f32)
        return total

    def level_gather(block, full, sem):
        def body(k, carry):
            peer = lax.rem(lv + k, nv)
            lev_copy(block, full.at[:, :, lanes(lv)], sem, peer).start()
            return carry

        lax.fori_loop(1, nv, body, 0)
        full[:, :, lanes(lv)] = block[...]

    def flat(ref):
        return ref[...].astype(f32).reshape(tokens, width)

    def blocks(values):
        return values.reshape(nl, m, width).astype(bf16)

    to_block = permutation(d, lat_to_block, True)
    loads[0].wait()
    send_t[...] = blocks(dot(to_block, tok_v[...]))
    loads[1].wait()
    send_f[...] = blocks(scale_ref[...] * dot(to_block, cot_v[...]))

    pl.semaphore_wait(barrier, nl - 1 + nv - 1)
    all_to_all(send_t, recv_t, 0)
    level_scatter(send_f, recv_f, 1)

    valid = mask_ref[...].astype(f32)
    for b in range(d.batch):
        row = jnp.concatenate([valid[b : b + 1]] * (QUAD // HEAD), axis=1)
        maskf[pl.ds(b * d.pl * d.lat, d.pl * d.lat), :] = jnp.broadcast_to(
            row, (d.pl * d.lat, d.keys)
        )

    send_fa[...] = level_sum(send_f, recv_f, 1).astype(bf16)
    all_to_all(send_fa, recv_fa, 2)

    all_to_all_done(send_t, recv_t, 0).wait_recv()
    x_group = dot(permutation(d, block_to_group, True), flat(recv_t).astype(bf16))
    xg[...] = x_group.astype(bf16)
    factor = lax.rsqrt(jnp.mean(x_group * x_group, axis=-1, keepdims=True) + epsilon)
    rx_s[...] = jnp.broadcast_to(factor, rx_s.shape)
    normed_s[...] = (x_group * factor).astype(bf16)

    all_to_all_done(send_fa, recv_fa, 2).wait_recv()
    level_gather(recv_fa, flow_full, 3)

    def same(shape, row_size, col_size):
        rows = lax.broadcasted_iota(jnp.int32, shape, 0) >> log2(row_size)
        cols = lax.broadcasted_iota(jnp.int32, shape, 1) >> log2(col_size)
        return jnp.where(rows == cols, 1.0, 0.0)

    def ones_e():
        return same((QUAD, QUAD), HEAD, HEAD).astype(bf16)

    def ones_k():
        return same((d.keys, d.keys), d.lat, d.lat).astype(bf16)

    def expand(block, spread):
        return jnp.concatenate([block] * (QUAD // HEAD), axis=0) * spread

    def collapse(product, spread):
        picked = product * spread
        total = picked[: d.lat]
        for h in range(1, QUAD // HEAD):
            total = total + picked[h * d.lat : (h + 1) * d.lat]
        return total

    groups = [slice(g * d.lat, (g + 1) * d.lat) for g in range(d.groups)]

    def head_mean(values, ones):
        return group_sum(values, ones) * (1.0 / HEAD)

    loads[2].wait()

    def columns(n, part):
        return pl.ds(pl.multiple_of(part * width + n * QUAD, QUAD), QUAD)

    def key_columns(n):
        return pl.ds(pl.multiple_of(n * d.keys, d.keys), d.keys)

    def forward_quad(n, carry):
        ones = ones_e()
        spread = same((d.keys, QUAD), d.lat, HEAD).astype(bf16)
        normed = normed_s[...]
        cast = []
        for part in range(2):
            raw = dot(normed, wq_v[:, columns(n, part)])
            fac = lax.rsqrt(head_mean(raw * raw, ones) + epsilon)
            raw_s[:, columns(n, part)] = raw
            fac_s[:, columns(n, part)] = fac
            cast.append((raw * fac).astype(bf16))
            qkv_s[:, columns(n, part)] = cast[part]
        value = dot(normed, wq_v[:, columns(n, 2)]).astype(bf16)
        qkv_s[:, columns(n, 2)] = value
        query, key = cast
        scores = jnp.concatenate(
            [dot_nt(query[g], expand(key[g], spread)) for g in groups], axis=0
        )
        exp_scores = jnp.exp(scores * score_scale) * maskf[...]
        attn = exp_scores / group_sum(exp_scores, ones_k())
        attn_s[:, key_columns(n)] = attn
        attn_b = attn.astype(bf16)
        attended = jnp.concatenate(
            [dot(attn_b[g], expand(value[g], spread)) for g in groups], axis=0
        )
        att_s[:, columns(n, 0)] = attended.astype(bf16)
        return carry

    lax.fori_loop(0, d.quads, forward_quad, 0)

    att_s[...] = dot(permutation(d, block_to_group, False), att_s[...]).astype(bf16)
    loads[3].wait()
    send_m[...] = blocks(dot(att_s[...], wm_v[...]))
    level_scatter(send_m, recv_m, 4)

    lev_copy(recv_f, recv_f, 3, lax.rem(lv + 1, nv)).wait_recv()
    flow_a[...] = flat(flow_full).astype(bf16)

    def mix_rows(n, carry):
        rows = pl.ds(pl.multiple_of(n * QUAD, QUAD), QUAD)
        part = dot_tn(att_s[:, rows], flow_a[...]) * d.grad_scale
        per = QUAD // (d.nx * d.out_rows)
        mg_s[pl.ds(n * per, per)] = part.astype(bf16).reshape(per, d.nx, d.out_rows, width)
        return carry

    lax.fori_loop(0, d.quads, mix_rows, 0)

    z_at = me >> log2(d.nx)
    x_at = me & (d.nx - 1)

    def scatter_x(k, carry):
        x_to = (x_at + k) & (d.nx - 1)
        lat_copy(mg_s.at[:, x_to], recv_g1.at[k - 1], 5, z_at * d.nx + x_to).start()
        return carry

    lax.fori_loop(1, d.nx, scatter_x, 0)

    flow_g[...] = dot(permutation(d, block_to_group, True), flow_a[...]).astype(bf16)

    def backward_quad(n, carry):
        ones = ones_e()
        spread = same((d.keys, QUAD), d.lat, HEAD)
        spread_b = spread.astype(bf16)
        rows = pl.ds(pl.multiple_of(n * QUAD, QUAD), QUAD)
        d_att = dot_nt(flow_g[...], wm_v[rows, :]).astype(bf16)
        query = qkv_s[:, columns(n, 0)]
        key = qkv_s[:, columns(n, 1)]
        value = qkv_s[:, columns(n, 2)]
        attn = attn_s[:, key_columns(n)]
        attn_b = attn.astype(bf16)
        d_attn = jnp.concatenate(
            [dot_nt(d_att[g], expand(value[g], spread_b)) for g in groups], axis=0
        )
        inner = group_sum(attn * d_attn, ones_k())
        d_scores = (attn * (d_attn - inner) * score_scale).astype(bf16)
        d_value = jnp.concatenate(
            [collapse(dot_tn(attn_b[g], d_att[g]), spread) for g in groups], axis=0
        )
        d_key = jnp.concatenate(
            [collapse(dot_tn(d_scores[g], query[g]), spread) for g in groups], axis=0
        )
        d_query = jnp.concatenate(
            [dot(d_scores[g], expand(key[g], spread_b)) for g in groups], axis=0
        )
        gp_s[:, columns(n, 2)] = d_value.astype(bf16)
        for part, upstream in ((0, d_query), (1, d_key)):
            up = upstream.astype(bf16).astype(f32)
            raw = raw_s[:, columns(n, part)]
            fac = fac_s[:, columns(n, part)]
            mean = head_mean(up * raw, ones)
            gp_s[:, columns(n, part)] = (fac * up - raw * (fac * fac * fac) * mean).astype(bf16)
        return carry

    half = d.quads // 2
    lax.fori_loop(0, half, backward_quad, 0)

    send_ma[...] = level_sum(send_m, recv_m, 4).astype(bf16)
    all_to_all(send_ma, recv_ma, 6)

    lax.fori_loop(half, d.quads, backward_quad, 0)

    all_to_all_done(send_ma, recv_ma, 6).wait_recv()
    level_gather(recv_ma, mix_full, 7)

    def project_back(n, carry):
        cols = pl.ds(pl.multiple_of(n * QUAD, QUAD), QUAD)
        dn_s[:, cols] = dot_nt(gp_s[...], wq_v[cols, :])
        return carry

    lax.fori_loop(0, d.quads, project_back, 0)

    x_group = xg[...].astype(f32)
    d_normed = dn_s[...]
    factor = rx_s[:, :1]
    mean = jnp.mean(d_normed * x_group, axis=-1, keepdims=True)
    d_group = (factor * d_normed - x_group * (factor * factor * factor * mean)).astype(bf16)
    send_d[...] = blocks(dot(permutation(d, block_to_group, False), d_group))
    all_to_all(send_d, recv_d, 8)

    lat_copy(recv_g1, recv_g1, 5, z_at * d.nx + ((x_at + 1) & (d.nx - 1))).wait_recv()

    def sum_x(n, carry):
        total = mg_s[n, x_at].astype(f32)
        for k in range(d.nx - 1):
            total = total + recv_g1[k, n].astype(f32)
        send_g2[n] = total.astype(bf16)
        return carry

    lax.fori_loop(0, d.nz, sum_x, 0)

    def scatter_z(k, carry):
        z_to = (z_at + k) & (d.nz - 1)
        lat_copy(send_g2.at[z_to], recv_g2.at[k - 1], 9, z_to * d.nx + x_at).start()
        return carry

    lax.fori_loop(1, d.nz, scatter_z, 0)

    to_lat = permutation(d, lat_to_block, False)
    lev_copy(recv_m, recv_m, 7, lax.rem(lv + 1, nv)).wait_recv()
    mixed = (flat(send_t) + scale_ref[...] * flat(mix_full)).astype(bf16)
    out_ref[...] = dot(to_lat, mixed).astype(bf16)

    all_to_all_done(send_d, recv_d, 8).wait_recv()
    d_lat = dot(to_lat, flat(recv_d).astype(bf16))
    dtok_ref[...] = (cot_v[...].astype(f32) + d_lat).astype(bf16)

    z_peer = ((z_at + 1) & (d.nz - 1)) * d.nx + x_at
    lat_copy(recv_g2, recv_g2, 9, z_peer).wait_recv()
    total = send_g2[z_at].astype(f32)
    for k in range(d.nz - 1):
        total = total + recv_g2[k].astype(f32)
    mg_ref[...] = total

    for send, recv, sem in (
        (send_t, recv_t, 0),
        (send_fa, recv_fa, 2),
        (send_ma, recv_ma, 6),
        (send_d, recv_d, 8),
    ):
        all_to_all_done(send, recv, sem).wait_send()
    lev_peer = lax.rem(lv + 1, nv)
    for ref, sem in ((recv_f, 1), (recv_f, 3), (recv_m, 4), (recv_m, 7)):
        lev_copy(ref, ref, sem, lev_peer).wait_send()
    lat_copy(recv_g1, recv_g1, 5, z_peer).wait_send()
    lat_copy(recv_g2, recv_g2, 9, z_peer).wait_send()


def on_device(x_chips, tokens, key_mask, w_qkv, w_mix, level_scale, cotangent):
    batch, _, band_rows, lon, width = tokens.shape
    nl, nv = lax.axis_size("lat"), lax.axis_size("lev")
    d = SimpleNamespace(
        nl=nl, nv=nv, batch=batch, rb=band_rows, lon=lon, width=width, pl=lon // nl,
        lat=nl * band_rows, tokens=batch * band_rows * lon, piece=width // nv,
        nx=x_chips, nz=nl // x_chips, quads=width // QUAD, out_rows=width // nl,
    )
    d.m = d.tokens // nl
    d.groups = batch * d.pl
    d.keys = (QUAD // HEAD) * d.lat
    d.grad_scale = 1.0 / math.sqrt(batch * d.lat * lon)
    flat_shape = (d.tokens, width)
    block = (nl, d.m, width)
    part = (nl, d.m, d.piece)
    parts = (nv - 1,) + part

    def vmem(shape, dtype=bf16):
        return pltpu.VMEM(shape, dtype)

    scratch = [
        vmem(flat_shape),
        vmem(flat_shape),
        vmem((width, 3 * width)),
        vmem((width, width)),
        vmem(block),
        vmem(block),
        vmem(block),
        vmem(parts),
        vmem(part),
        vmem(part),
        vmem(block),
        vmem(block),
        vmem(parts),
        vmem(part),
        vmem(part),
        vmem(block),
        vmem(block),
        vmem(block),
        vmem((d.nz, d.nx, d.out_rows, width)),
        vmem((d.nx - 1, d.nz, d.out_rows, width)),
        vmem((d.nz, d.out_rows, width)),
        vmem((d.nz - 1, d.out_rows, width)),
        vmem(flat_shape),
        vmem((d.tokens, 128), f32),
        vmem(flat_shape),
        vmem((d.tokens, 2 * width), f32),
        vmem((d.tokens, 2 * width), f32),
        vmem((d.tokens, 3 * width)),
        vmem((d.tokens, d.quads * d.keys), f32),
        vmem(flat_shape),
        vmem(flat_shape),
        vmem(flat_shape),
        vmem((d.tokens, 3 * width)),
        vmem(flat_shape, f32),
        vmem((d.tokens, d.keys), f32),
        pltpu.SemaphoreType.DMA((4,)),
        pltpu.SemaphoreType.DMA((10,)),
        pltpu.SemaphoreType.DMA((10,)),
    ]
    any_space = pl.BlockSpec(memory_space=pl.ANY)
    in_vmem = pl.BlockSpec(memory_space=pltpu.VMEM)
    output, d_tokens, mix_grad = pl.pallas_call(
        functools.partial(kernel, d),
        name="latitude_block",
        out_shape=(
            jax.ShapeDtypeStruct(flat_shape, bf16),
            jax.ShapeDtypeStruct(flat_shape, bf16),
            jax.ShapeDtypeStruct((d.out_rows, width), f32),
        ),
        in_specs=[any_space, in_vmem, any_space, any_space, in_vmem, any_space],
        out_specs=(in_vmem, in_vmem, in_vmem),
        scratch_shapes=scratch,
        compiler_params=pltpu.CompilerParams(
            collective_id=0, has_side_effects=True, vmem_limit_bytes=60 * 1024 * 1024
        ),
    )(
        tokens.reshape(flat_shape),
        key_mask,
        w_qkv,
        w_mix.reshape(width, width),
        level_scale,
        cotangent.reshape(flat_shape),
    )
    return (
        output.reshape(tokens.shape),
        d_tokens.reshape(tokens.shape),
        mix_grad.reshape(1, d.out_rows, width),
    )


def solution(mesh, x_chips=X_CHIPS):
    return jax.shard_map(
        functools.partial(on_device, x_chips),
        mesh=mesh,
        in_specs=(
            P(None, "lev", "lat", None, None),
            P(),
            P(),
            P("lev", None, None),
            P("lev", None),
            P(None, "lev", "lat", None, None),
        ),
        out_specs=(
            P(None, "lev", "lat", None, None),
            P(None, "lev", "lat", None, None),
            P("lev", "lat", None),
        ),
        check_vma=False,
    )
```

```python
import functools
import math
from types import SimpleNamespace

import jax
import jax.numpy as jnp
from jax import lax
from jax.experimental import pallas as pl
from jax.experimental.pallas import tpu as pltpu
from jax.sharding import PartitionSpec as P

HEAD = 64
QUAD = 256
X_CHIPS = 4
epsilon = 1e-06
score_scale = 0.25
f32 = jnp.float32
bf16 = jnp.bfloat16
MESH = pl.DeviceIdType.MESH


def dot(a, b):
    return lax.dot_general(a, b, (((1,), (0,)), ((), ())), preferred_element_type=f32)


def dot_nt(a, b):
    return lax.dot_general(a, b, (((1,), (1,)), ((), ())), preferred_element_type=f32)


def dot_tn(a, b):
    return lax.dot_general(a, b, (((0,), (0,)), ((), ())), preferred_element_type=f32)


def log2(n):
    return n.bit_length() - 1


def lat_to_block(d, a):
    j = a >> log2(d.m)
    b = (a >> log2(d.rb * d.pl)) & (d.batch - 1)
    r = (a >> log2(d.pl)) & (d.rb - 1)
    p = a & (d.pl - 1)
    return (b * d.rb + r) * d.lon + j * d.pl + p


def block_to_group(d, c):
    b = c >> log2(d.pl * d.lat)
    p = (c >> log2(d.lat)) & (d.pl - 1)
    i = (c & (d.lat - 1)) >> log2(d.rb)
    r = c & (d.rb - 1)
    return i * d.m + b * d.rb * d.pl + r * d.pl + p


def permutation(d, index, forward):
    rows = lax.broadcasted_iota(jnp.int32, (d.tokens, d.tokens), 0)
    cols = lax.broadcasted_iota(jnp.int32, (d.tokens, d.tokens), 1)
    hit = index(d, rows) == cols if forward else index(d, cols) == rows
    return jnp.where(hit, 1.0, 0.0).astype(bf16)


def group_sum(values, ones):
    high = values.astype(bf16)
    low = (values - high.astype(f32)).astype(bf16)
    return dot(high, ones) + dot(low, ones)


def kernel(
    d,
    tok_hbm,
    mask_ref,
    wq_hbm,
    wm_hbm,
    scale_ref,
    cot_hbm,
    out_ref,
    dtok_ref,
    mg_ref,
    tok_v,
    cot_v,
    wq_v,
    wm_v,
    send_t,
    recv_t,
    send_f,
    recv_fp,
    sum_f,
    recv_f,
    send_fa,
    recv_fa,
    flow_full,
    send_m,
    recv_mp,
    sum_m,
    recv_m,
    send_ma,
    recv_ma,
    mix_full,
    send_d,
    recv_d,
    mg_s,
    recv_ga,
    recv_gb,
    send_g2,
    recv_g2,
    xg,
    rx_s,
    normed_s,
    raw_s,
    fac_s,
    qkv_s,
    attn_s,
    att_s,
    flow_a,
    flow_g,
    gp_s,
    dn_s,
    maskf,
    load_sem,
    send_sem,
    recv_sem,
):
    me = lax.axis_index("lat")
    lv = lax.axis_index("lev")
    nl, nv, m, width, tokens = d.nl, d.nv, d.m, d.width, d.tokens
    ny = nv // 2
    piece = d.piece
    loads = [
        pltpu.make_async_copy(src, dst, load_sem.at[n])
        for n, (src, dst) in enumerate(
            ((tok_hbm, tok_v), (cot_hbm, cot_v), (wq_hbm, wq_v), (wm_hbm, wm_v))
        )
    ]
    for load in loads:
        load.start()

    barrier = pltpu.get_barrier_semaphore()

    def greet_lat(k, carry):
        pl.semaphore_signal(
            barrier, inc=1, device_id={"lat": lax.rem(me + k, nl)}, device_id_type=MESH
        )
        return carry

    lax.fori_loop(1, nl, greet_lat, 0)
    pl.semaphore_signal(barrier, inc=1, device_id={"lev": lv ^ 1}, device_id_type=MESH)
    for k in range(1, ny):
        y_to = ((lv >> 1) + k) & (ny - 1)
        pl.semaphore_signal(
            barrier, inc=1, device_id={"lev": y_to * 2 + (lv & 1)}, device_id_type=MESH
        )

    def lat_copy(src, dst, sem, peer, recv=None):
        return pltpu.make_async_remote_copy(
            src_ref=src,
            dst_ref=dst,
            send_sem=send_sem.at[sem],
            recv_sem=recv_sem.at[sem if recv is None else recv],
            device_id={"lat": peer},
            device_id_type=MESH,
        )

    def lev_copy(src, dst, sem, peer):
        return pltpu.make_async_remote_copy(
            src_ref=src,
            dst_ref=dst,
            send_sem=send_sem.at[sem],
            recv_sem=recv_sem.at[sem],
            device_id={"lev": peer},
            device_id_type=MESH,
        )

    def all_to_all(send, recv, sem):
        def body(k, carry):
            peer = lax.rem(me + k, nl)
            lat_copy(send.at[peer], recv.at[me], sem, peer).start()
            return carry

        lax.fori_loop(1, nl, body, 0)
        recv[me] = send[me]

    def all_to_all_done(send, recv, sem):
        return lat_copy(
            send.at[pl.ds(0, nl - 1)], recv.at[pl.ds(0, nl - 1)], sem, lax.rem(me + 1, nl)
        )

    y_at, core = lv >> 1, lv & 1
    partner = lv ^ 1
    own_piece = core * ny + y_at
    mine, other = pl.ds(core * ny, ny), pl.ds((1 - core) * ny, ny)
    next_y = ((y_at + 1) & (ny - 1)) * 2 + core

    def scatter_pair(send, recv_p, sem):
        lev_copy(send.at[other], recv_p, sem, partner).start()

    def scatter_ring(send, recv_p, pair_sem, part_sum, recv, sem):
        lev_copy(recv_p, recv_p, pair_sem, partner).wait_recv()
        part_sum[...] = (send[mine].astype(f32) + recv_p[...].astype(f32)).astype(bf16)
        for k in range(1, ny):
            y_to = (y_at + k) & (ny - 1)
            lev_copy(part_sum.at[y_to], recv.at[k - 1], sem, y_to * 2 + core).start()

    def level_sum(part_sum, recv, sem):
        lev_copy(recv, recv, sem, next_y).wait_recv()
        total = part_sum[y_at].astype(f32)
        for k in range(ny - 1):
            total = total + recv[k].astype(f32)
        return total

    def gather_ring(block, full, sem):
        for k in range(1, ny):
            y_to = (y_at + k) & (ny - 1)
            lev_copy(block, full.at[own_piece], sem, y_to * 2 + core).start()
        full[own_piece] = block[...]

    def gather_pair(full, recv, ring_sem, sem):
        lev_copy(recv, recv, ring_sem, next_y).wait_recv()
        lev_copy(full.at[mine], full.at[mine], sem, partner).start()

    def flat(ref):
        return ref[...].astype(f32).reshape(tokens, width)

    def blocks(values):
        return values.reshape(nl, m, width).astype(bf16)

    def store_pieces(ref, values):
        for q in range(nv):
            part = values[:, q * piece : (q + 1) * piece]
            ref[q] = part.reshape(nl, m, piece).astype(bf16)

    def load_pieces(ref):
        parts = [ref[q].astype(f32).reshape(tokens, piece) for q in range(nv)]
        return jnp.concatenate(parts, axis=1)

    to_block = permutation(d, lat_to_block, True)
    loads[0].wait()
    send_t[...] = blocks(dot(to_block, tok_v[...]))
    loads[1].wait()
    store_pieces(send_f, scale_ref[...] * dot(to_block, cot_v[...]))

    pl.semaphore_wait(barrier, nl - 1 + ny)
    scatter_pair(send_f, recv_fp, 1)
    all_to_all(send_t, recv_t, 0)

    valid = mask_ref[...].astype(f32)
    for b in range(d.batch):
        row = jnp.concatenate([valid[b : b + 1]] * (QUAD // HEAD), axis=1)
        maskf[pl.ds(b * d.pl * d.lat, d.pl * d.lat), :] = jnp.broadcast_to(
            row, (d.pl * d.lat, d.keys)
        )

    scatter_ring(send_f, recv_fp, 1, sum_f, recv_f, 11)
    send_fa[...] = level_sum(sum_f, recv_f, 11).astype(bf16)
    all_to_all(send_fa, recv_fa, 2)

    all_to_all_done(send_t, recv_t, 0).wait_recv()
    x_group = dot(permutation(d, block_to_group, True), flat(recv_t).astype(bf16))
    xg[...] = x_group.astype(bf16)
    factor = lax.rsqrt(jnp.mean(x_group * x_group, axis=-1, keepdims=True) + epsilon)
    rx_s[...] = jnp.broadcast_to(factor, rx_s.shape)
    normed_s[...] = (x_group * factor).astype(bf16)

    all_to_all_done(send_fa, recv_fa, 2).wait_recv()
    gather_ring(recv_fa, flow_full, 3)

    def same(shape, row_size, col_size):
        rows = lax.broadcasted_iota(jnp.int32, shape, 0) >> log2(row_size)
        cols = lax.broadcasted_iota(jnp.int32, shape, 1) >> log2(col_size)
        return jnp.where(rows == cols, 1.0, 0.0)

    def ones_e():
        return same((QUAD, QUAD), HEAD, HEAD).astype(bf16)

    def ones_k():
        return same((d.keys, d.keys), d.lat, d.lat).astype(bf16)

    def expand(block, spread):
        return jnp.concatenate([block] * (QUAD // HEAD), axis=0) * spread

    def collapse(product, spread):
        picked = product * spread
        total = picked[: d.lat]
        for h in range(1, QUAD // HEAD):
            total = total + picked[h * d.lat : (h + 1) * d.lat]
        return total

    groups = [slice(g * d.lat, (g + 1) * d.lat) for g in range(d.groups)]

    def head_mean(values, ones):
        return group_sum(values, ones) * (1.0 / HEAD)

    loads[2].wait()

    def columns(n, part):
        start = part * width + n * QUAD
        return pl.ds(start if isinstance(n, int) else pl.multiple_of(start, QUAD), QUAD)

    def key_columns(n):
        return pl.ds(n * d.keys if isinstance(n, int) else pl.multiple_of(n * d.keys, d.keys), d.keys)

    def forward_quad(n, carry):
        ones = ones_e()
        spread = same((d.keys, QUAD), d.lat, HEAD).astype(bf16)
        normed = normed_s[...]
        cast = []
        for part in range(2):
            raw = dot(normed, wq_v[:, columns(n, part)])
            fac = lax.rsqrt(head_mean(raw * raw, ones) + epsilon)
            raw_s[:, columns(n, part)] = raw
            fac_s[:, columns(n, part)] = fac
            cast.append((raw * fac).astype(bf16))
            qkv_s[:, columns(n, part)] = cast[part]
        value = dot(normed, wq_v[:, columns(n, 2)]).astype(bf16)
        qkv_s[:, columns(n, 2)] = value
        query, key = cast
        scores = jnp.concatenate(
            [dot_nt(query[g], expand(key[g], spread)) for g in groups], axis=0
        )
        exp_scores = jnp.exp(scores * score_scale) * maskf[...]
        attn = exp_scores / group_sum(exp_scores, ones_k())
        attn_s[:, key_columns(n)] = attn
        attn_b = attn.astype(bf16)
        attended = jnp.concatenate(
            [dot(attn_b[g], expand(value[g], spread)) for g in groups], axis=0
        )
        att_s[:, columns(n, 0)] = attended.astype(bf16)
        return carry

    lax.fori_loop(0, d.quads // 2, forward_quad, 0)
    gather_pair(flow_full, recv_f, 3, 12)
    lax.fori_loop(d.quads // 2, d.quads, forward_quad, 0)

    att_s[...] = dot(permutation(d, block_to_group, False), att_s[...]).astype(bf16)
    loads[3].wait()
    store_pieces(send_m, dot(att_s[...], wm_v[...]))
    scatter_pair(send_m, recv_mp, 4)

    lev_copy(recv_fp, recv_fp, 12, partner).wait_recv()
    flow_a[...] = load_pieces(flow_full).astype(bf16)

    z_at = me >> log2(d.nx)
    x_at = me & (d.nx - 1)
    x_next, x_prev = (x_at + 1) & (d.nx - 1), (x_at - 1) & (d.nx - 1)
    x_far = (x_at + 2) & (d.nx - 1)
    half_rows = d.out_rows // 2
    top, bottom = pl.ds(0, half_rows), pl.ds(half_rows, half_rows)
    sides = ((x_next, top, 0), (x_prev, bottom, 1))
    offsets = sorted(range(d.chunks), key=lambda o: -min(o, d.chunks - o))

    def chunk_of(step):
        return ((z_at >> log2(d.per)) + offsets[step]) & (d.chunks - 1)

    def chunk_rows(step):
        return pl.ds(chunk_of(step) * d.per, d.per)

    def column(x):
        return z_at * d.nx + x

    def far_copy(step, x_to, rows, side):
        return lat_copy(
            mg_s.at[chunk_rows(step), x_far, rows], recv_ga.at[side, step], 5, column(x_to),
            15 + side * d.chunks + step,
        )

    def near_copy(step, x_to, side):
        return lat_copy(
            mg_s.at[chunk_rows(step), x_to], recv_gb.at[side, step], 9, column(x_to),
            15 + (2 + side) * d.chunks + step,
        )

    def mix_chunk(step):
        start = pl.multiple_of(chunk_of(step) * QUAD, QUAD)
        part = dot_tn(att_s[:, pl.ds(start, QUAD)], flow_a[...]) * d.grad_scale
        mg_s[chunk_rows(step)] = part.astype(bf16).reshape(d.per, d.nx, d.out_rows, width)
        for x_to, rows, side in sides:
            far_copy(step, x_to, rows, side).start()

    def relay_chunk(step):
        for x_to, rows, side in sides:
            far_copy(step, x_to, rows, side).wait_recv()
            mine = mg_s[chunk_rows(step), x_to, rows].astype(f32)
            mine = mine + recv_ga[side, step].astype(f32)
            mg_s[chunk_rows(step), x_to, rows] = mine.astype(bf16)
            near_copy(step, x_to, side).start()

    def finish_chunk(step):
        total = mg_s[chunk_rows(step), x_at].astype(f32)
        for x_to, rows, side in sides:
            near_copy(step, x_to, side).wait_recv()
            total = total + recv_gb[side, step].astype(f32)
        send_g2[chunk_rows(step)] = total.astype(bf16)
        for n in range(d.per):
            if offsets[step] == 0:
                if n == 0:
                    continue
                z_to = z_at ^ n
            else:
                z_to = chunk_of(step) * d.per + n
            slot = ((z_to - z_at) & (d.nz - 1)) - 1
            lat_copy(send_g2.at[z_to], recv_g2.at[slot], 10, z_to * d.nx + x_at, 9).start()

    for step in range(d.chunks):
        if step == d.chunks // 2:
            scatter_ring(send_m, recv_mp, 4, sum_m, recv_m, 13)
        mix_chunk(step)

    flow_g[...] = dot(permutation(d, block_to_group, True), flow_a[...]).astype(bf16)

    def backward_quad(n, carry):
        ones = ones_e()
        spread = same((d.keys, QUAD), d.lat, HEAD)
        spread_b = spread.astype(bf16)
        rows = columns(n, 0)
        d_att = dot_nt(flow_g[...], wm_v[rows, :]).astype(bf16)
        query = qkv_s[:, columns(n, 0)]
        key = qkv_s[:, columns(n, 1)]
        value = qkv_s[:, columns(n, 2)]
        attn = attn_s[:, key_columns(n)]
        attn_b = attn.astype(bf16)
        d_attn = jnp.concatenate(
            [dot_nt(d_att[g], expand(value[g], spread_b)) for g in groups], axis=0
        )
        inner = group_sum(attn * d_attn, ones_k())
        d_scores = (attn * (d_attn - inner) * score_scale).astype(bf16)
        d_value = jnp.concatenate(
            [collapse(dot_tn(attn_b[g], d_att[g]), spread) for g in groups], axis=0
        )
        d_key = jnp.concatenate(
            [collapse(dot_tn(d_scores[g], query[g]), spread) for g in groups], axis=0
        )
        d_query = jnp.concatenate(
            [dot(d_scores[g], expand(key[g], spread_b)) for g in groups], axis=0
        )
        gp_s[:, columns(n, 2)] = d_value.astype(bf16)
        for part, upstream in ((0, d_query), (1, d_key)):
            up = upstream.astype(bf16).astype(f32)
            raw = raw_s[:, columns(n, part)]
            fac = fac_s[:, columns(n, part)]
            mean = head_mean(up * raw, ones)
            gp_s[:, columns(n, part)] = (fac * up - raw * (fac * fac * fac) * mean).astype(bf16)
        return carry

    for n in range(d.quads):
        if n == d.quads - 1:
            send_ma[...] = level_sum(sum_m, recv_m, 13).astype(bf16)
            all_to_all(send_ma, recv_ma, 6)
        backward_quad(n, 0)
        relay_chunk(n)

    def project_back(n, carry):
        cols = pl.ds(pl.multiple_of(n * QUAD, QUAD), QUAD)
        dn_s[:, cols] = dot_nt(gp_s[...], wq_v[cols, :])
        return carry

    lax.fori_loop(0, d.quads, project_back, 0)

    x_group = xg[...].astype(f32)
    d_normed = dn_s[...]
    factor = rx_s[:, :1]
    mean = jnp.mean(d_normed * x_group, axis=-1, keepdims=True)
    d_group = (factor * d_normed - x_group * (factor * factor * factor * mean)).astype(bf16)
    send_d[...] = blocks(dot(permutation(d, block_to_group, False), d_group))
    all_to_all(send_d, recv_d, 8)

    all_to_all_done(send_ma, recv_ma, 6).wait_recv()
    gather_ring(recv_ma, mix_full, 7)
    for step in range(d.chunks):
        if step == d.chunks // 2:
            gather_pair(mix_full, recv_m, 7, 14)
        finish_chunk(step)

    to_lat = permutation(d, lat_to_block, False)
    lev_copy(recv_mp, recv_mp, 14, partner).wait_recv()
    mixed = (flat(send_t) + scale_ref[...] * load_pieces(mix_full)).astype(bf16)
    out_ref[...] = dot(to_lat, mixed).astype(bf16)

    all_to_all_done(send_d, recv_d, 8).wait_recv()
    d_lat = dot(to_lat, flat(recv_d).astype(bf16))
    dtok_ref[...] = (cot_v[...].astype(f32) + d_lat).astype(bf16)

    z_peer = ((z_at + 1) & (d.nz - 1)) * d.nx + x_at
    lat_copy(recv_g2, recv_g2, 10, z_peer, 9).wait_recv()
    total = send_g2[z_at].astype(f32)
    for k in range(d.nz - 1):
        total = total + recv_g2[k].astype(f32)
    mg_ref[...] = total

    for send, recv, sem in (
        (send_t, recv_t, 0),
        (send_fa, recv_fa, 2),
        (send_ma, recv_ma, 6),
        (send_d, recv_d, 8),
    ):
        all_to_all_done(send, recv, sem).wait_send()
    for pair_ref, ring_ref, sems in (
        (recv_fp, recv_f, (1, 11, 3, 12)),
        (recv_mp, recv_m, (4, 13, 7, 14)),
    ):
        for sem, ref in zip(sems, (pair_ref, ring_ref, ring_ref, pair_ref)):
            lev_copy(ref, ref, sem, partner).wait_send()
    for ref, sem in ((recv_ga, 5), (recv_gb, 9), (recv_g2, 10)):
        lat_copy(ref, ref, sem, z_peer, 9).wait_send()


def hand_over(*refs):
    for src, dst in zip(refs[:3], refs[3:]):
        dst[...] = src[...]


def on_device(x_chips, tokens, key_mask, w_qkv, w_mix, level_scale, cotangent):
    batch, _, band_rows, lon, width = tokens.shape
    nl, nv = lax.axis_size("lat"), lax.axis_size("lev")
    d = SimpleNamespace(
        nl=nl, nv=nv, batch=batch, rb=band_rows, lon=lon, width=width, pl=lon // nl,
        lat=nl * band_rows, tokens=batch * band_rows * lon, piece=width // nv,
        nx=x_chips, nz=nl // x_chips, quads=width // QUAD, out_rows=width // nl,
    )
    d.m = d.tokens // nl
    d.groups = batch * d.pl
    d.keys = (QUAD // HEAD) * d.lat
    d.per = QUAD // (d.nx * d.out_rows)
    d.chunks = d.nz // d.per
    d.grad_scale = 1.0 / math.sqrt(batch * d.lat * lon)
    flat_shape = (d.tokens, width)
    block = (nl, d.m, width)
    part = (nl, d.m, d.piece)
    half = (nv // 2,) + part
    parts = (nv // 2 - 1,) + part
    whole = (nv,) + part

    def vmem(shape, dtype=bf16):
        return pltpu.VMEM(shape, dtype)

    scratch = [
        vmem(flat_shape),
        vmem(flat_shape),
        vmem((width, 3 * width)),
        vmem((width, width)),
        vmem(block),
        vmem(block),
        vmem(whole),
        vmem(half),
        vmem(half),
        vmem(parts),
        vmem(part),
        vmem(part),
        vmem(whole),
        vmem(whole),
        vmem(half),
        vmem(half),
        vmem(parts),
        vmem(part),
        vmem(part),
        vmem(whole),
        vmem(block),
        vmem(block),
        vmem((d.nz, d.nx, d.out_rows, width)),
        vmem((2, d.chunks, d.per, d.out_rows // 2, width)),
        vmem((2, d.chunks, d.per, d.out_rows, width)),
        vmem((d.nz, d.out_rows, width)),
        vmem((d.nz - 1, d.out_rows, width)),
        vmem(flat_shape),
        vmem((d.tokens, 128), f32),
        vmem(flat_shape),
        vmem((d.tokens, 2 * width), f32),
        vmem((d.tokens, 2 * width), f32),
        vmem((d.tokens, 3 * width)),
        vmem((d.tokens, d.quads * d.keys), f32),
        vmem(flat_shape),
        vmem(flat_shape),
        vmem(flat_shape),
        vmem((d.tokens, 3 * width)),
        vmem(flat_shape, f32),
        vmem((d.tokens, d.keys), f32),
        pltpu.SemaphoreType.DMA((4,)),
        pltpu.SemaphoreType.DMA((15,)),
        pltpu.SemaphoreType.DMA((15 + 4 * d.chunks,)),
    ]
    any_space = pl.BlockSpec(memory_space=pl.ANY)
    in_vmem = pl.BlockSpec(memory_space=pltpu.VMEM)
    results = pl.pallas_call(
        functools.partial(kernel, d),
        name="latitude_block",
        out_shape=(
            jax.ShapeDtypeStruct(flat_shape, bf16),
            jax.ShapeDtypeStruct(flat_shape, bf16),
            jax.ShapeDtypeStruct((d.out_rows, width), f32),
        ),
        in_specs=[any_space, in_vmem, any_space, any_space, in_vmem, any_space],
        out_specs=(in_vmem, in_vmem, in_vmem),
        scratch_shapes=scratch,
        compiler_params=pltpu.CompilerParams(
            collective_id=0, has_side_effects=True, vmem_limit_bytes=60 * 1024 * 1024
        ),
    )(
        tokens.reshape(flat_shape),
        key_mask,
        w_qkv,
        w_mix.reshape(width, width),
        level_scale,
        cotangent.reshape(flat_shape),
    )
    output, d_tokens, mix_grad = pl.pallas_call(
        hand_over,
        name="hand_over",
        out_shape=tuple(jax.ShapeDtypeStruct(x.shape, x.dtype) for x in results),
        in_specs=[in_vmem] * 3,
        out_specs=(in_vmem,) * 3,
    )(*results)
    return (
        output.reshape(tokens.shape),
        d_tokens.reshape(tokens.shape),
        mix_grad.reshape(1, d.out_rows, width),
    )


def solution(mesh, x_chips=X_CHIPS):
    return jax.shard_map(
        functools.partial(on_device, x_chips),
        mesh=mesh,
        in_specs=(
            P(None, "lev", "lat", None, None),
            P(),
            P(),
            P("lev", None, None),
            P("lev", None),
            P(None, "lev", "lat", None, None),
        ),
        out_specs=(
            P(None, "lev", "lat", None, None),
            P(None, "lev", "lat", None, None),
            P("lev", "lat", None),
        ),
        check_vma=False,
    )
```

```python
import functools
import math
from types import SimpleNamespace

import jax
import jax.numpy as jnp
from jax import lax
from jax.experimental import pallas as pl
from jax.experimental.pallas import tpu as pltpu
from jax.sharding import PartitionSpec as P

HEAD = 64
QUAD = 256
X_CHIPS = 4
epsilon = 1e-06
score_scale = 0.25
f32 = jnp.float32
bf16 = jnp.bfloat16
MESH = pl.DeviceIdType.MESH


def dot(a, b):
    return lax.dot_general(a, b, (((1,), (0,)), ((), ())), preferred_element_type=f32)


def dot_nt(a, b):
    return lax.dot_general(a, b, (((1,), (1,)), ((), ())), preferred_element_type=f32)


def dot_tn(a, b):
    return lax.dot_general(a, b, (((0,), (0,)), ((), ())), preferred_element_type=f32)


def log2(n):
    return n.bit_length() - 1


def lat_to_block(d, a):
    j = a >> log2(d.m)
    b = (a >> log2(d.rb * d.pl)) & (d.batch - 1)
    r = (a >> log2(d.pl)) & (d.rb - 1)
    p = a & (d.pl - 1)
    return (b * d.rb + r) * d.lon + j * d.pl + p


def block_to_group(d, c):
    b = c >> log2(d.pl * d.lat)
    p = (c >> log2(d.lat)) & (d.pl - 1)
    i = (c & (d.lat - 1)) >> log2(d.rb)
    r = c & (d.rb - 1)
    return i * d.m + b * d.rb * d.pl + r * d.pl + p


def permutation(d, index, forward):
    rows = lax.broadcasted_iota(jnp.int32, (d.tokens, d.tokens), 0)
    cols = lax.broadcasted_iota(jnp.int32, (d.tokens, d.tokens), 1)
    hit = index(d, rows) == cols if forward else index(d, cols) == rows
    return jnp.where(hit, 1.0, 0.0).astype(bf16)


def group_sum(values, ones):
    return dot(values.astype(bf16), ones)


def kernel(
    d,
    tok_hbm,
    mask_ref,
    wq_hbm,
    wm_hbm,
    scale_ref,
    cot_hbm,
    out_ref,
    dtok_ref,
    mg_ref,
    tok_v,
    cot_v,
    wq_v,
    wm_v,
    send_t,
    recv_t,
    send_f,
    recv_fp,
    sum_f,
    recv_f,
    send_fa,
    recv_fa,
    flow_full,
    send_m,
    recv_mp,
    sum_m,
    recv_m,
    send_ma,
    recv_ma,
    mix_full,
    send_d,
    recv_d,
    mg_s,
    recv_ga,
    recv_gb,
    send_g2,
    recv_g2,
    xg,
    rx_s,
    normed_s,
    raw_s,
    fac_s,
    qkv_s,
    attn_s,
    att_s,
    flow_a,
    flow_g,
    gp_s,
    dn_s,
    maskf,
    load_sem,
    send_sem,
    recv_sem,
):
    me = lax.axis_index("lat")
    lv = lax.axis_index("lev")
    nl, nv, m, width, tokens = d.nl, d.nv, d.m, d.width, d.tokens
    ny = nv // 2
    piece = d.piece
    loads = [
        pltpu.make_async_copy(src, dst, load_sem.at[n])
        for n, (src, dst) in enumerate(
            ((tok_hbm, tok_v), (cot_hbm, cot_v), (wq_hbm, wq_v), (wm_hbm, wm_v))
        )
    ]
    for load in loads:
        load.start()

    barrier = pltpu.get_barrier_semaphore()

    def greet_lat(k, carry):
        pl.semaphore_signal(
            barrier, inc=1, device_id={"lat": lax.rem(me + k, nl)}, device_id_type=MESH
        )
        return carry

    lax.fori_loop(1, nl, greet_lat, 0)
    pl.semaphore_signal(barrier, inc=1, device_id={"lev": lv ^ 1}, device_id_type=MESH)
    for k in range(1, ny):
        y_to = ((lv >> 1) + k) & (ny - 1)
        pl.semaphore_signal(
            barrier, inc=1, device_id={"lev": y_to * 2 + (lv & 1)}, device_id_type=MESH
        )

    def lat_copy(src, dst, sem, peer, recv=None):
        return pltpu.make_async_remote_copy(
            src_ref=src,
            dst_ref=dst,
            send_sem=send_sem.at[sem],
            recv_sem=recv_sem.at[sem if recv is None else recv],
            device_id={"lat": peer},
            device_id_type=MESH,
        )

    def lev_copy(src, dst, sem, peer):
        return pltpu.make_async_remote_copy(
            src_ref=src,
            dst_ref=dst,
            send_sem=send_sem.at[sem],
            recv_sem=recv_sem.at[sem],
            device_id={"lev": peer},
            device_id_type=MESH,
        )

    def all_to_all(send, recv, sem):
        def body(k, carry):
            peer = lax.rem(me + k, nl)
            lat_copy(send.at[peer], recv.at[me], sem, peer).start()
            return carry

        lax.fori_loop(1, nl, body, 0)
        recv[me] = send[me]

    def all_to_all_done(send, recv, sem):
        return lat_copy(
            send.at[pl.ds(0, nl - 1)], recv.at[pl.ds(0, nl - 1)], sem, lax.rem(me + 1, nl)
        )

    y_at, core = lv >> 1, lv & 1
    partner = lv ^ 1
    own_piece = core * ny + y_at
    mine, other = pl.ds(core * ny, ny), pl.ds((1 - core) * ny, ny)
    next_y = ((y_at + 1) & (ny - 1)) * 2 + core

    def scatter_pair(send, recv_p, sem):
        lev_copy(send.at[other], recv_p, sem, partner).start()

    def scatter_ring(send, recv_p, pair_sem, part_sum, recv, sem):
        lev_copy(recv_p, recv_p, pair_sem, partner).wait_recv()
        part_sum[...] = (send[mine].astype(f32) + recv_p[...].astype(f32)).astype(bf16)
        for k in range(1, ny):
            y_to = (y_at + k) & (ny - 1)
            lev_copy(part_sum.at[y_to], recv.at[k - 1], sem, y_to * 2 + core).start()

    def level_sum(part_sum, recv, sem):
        lev_copy(recv, recv, sem, next_y).wait_recv()
        total = part_sum[y_at].astype(f32)
        for k in range(ny - 1):
            total = total + recv[k].astype(f32)
        return total

    def gather_ring(block, full, sem):
        for k in range(1, ny):
            y_to = (y_at + k) & (ny - 1)
            lev_copy(block, full.at[own_piece], sem, y_to * 2 + core).start()
        full[own_piece] = block[...]

    def gather_pair(full, recv, ring_sem, sem):
        lev_copy(recv, recv, ring_sem, next_y).wait_recv()
        lev_copy(full.at[mine], full.at[mine], sem, partner).start()

    def flat(ref):
        return ref[...].astype(f32).reshape(tokens, width)

    def blocks(values):
        return values.reshape(nl, m, width).astype(bf16)

    def store_pieces(ref, values):
        for q in range(nv):
            part = values[:, q * piece : (q + 1) * piece]
            ref[q] = part.reshape(nl, m, piece).astype(bf16)

    def load_pieces(ref):
        parts = [ref[q].astype(f32).reshape(tokens, piece) for q in range(nv)]
        return jnp.concatenate(parts, axis=1)

    to_block = permutation(d, lat_to_block, True)
    loads[0].wait()
    send_t[...] = blocks(dot(to_block, tok_v[...]))
    loads[1].wait()
    store_pieces(send_f, scale_ref[...] * dot(to_block, cot_v[...]))

    pl.semaphore_wait(barrier, nl - 1 + ny)
    scatter_pair(send_f, recv_fp, 1)
    all_to_all(send_t, recv_t, 0)

    valid = mask_ref[...].astype(f32)
    for b in range(d.batch):
        row = jnp.concatenate([valid[b : b + 1]] * (QUAD // HEAD), axis=1)
        maskf[pl.ds(b * d.pl * d.lat, d.pl * d.lat), :] = jnp.broadcast_to(
            row, (d.pl * d.lat, d.keys)
        )

    scatter_ring(send_f, recv_fp, 1, sum_f, recv_f, 11)
    send_fa[...] = level_sum(sum_f, recv_f, 11).astype(bf16)
    all_to_all(send_fa, recv_fa, 2)

    all_to_all_done(send_t, recv_t, 0).wait_recv()
    x_group = dot(permutation(d, block_to_group, True), flat(recv_t).astype(bf16))
    xg[...] = x_group.astype(bf16)
    factor = lax.rsqrt(jnp.mean(x_group * x_group, axis=-1, keepdims=True) + epsilon)
    rx_s[...] = jnp.broadcast_to(factor, rx_s.shape)
    normed_s[...] = (x_group * factor).astype(bf16)

    all_to_all_done(send_fa, recv_fa, 2).wait_recv()
    gather_ring(recv_fa, flow_full, 3)

    def same(shape, row_size, col_size):
        rows = lax.broadcasted_iota(jnp.int32, shape, 0) >> log2(row_size)
        cols = lax.broadcasted_iota(jnp.int32, shape, 1) >> log2(col_size)
        return jnp.where(rows == cols, 1.0, 0.0)

    def ones_e():
        return same((QUAD, QUAD), HEAD, HEAD).astype(bf16)

    def ones_k():
        return same((d.keys, d.keys), d.lat, d.lat).astype(bf16)

    def expand(block, spread):
        return jnp.concatenate([block] * (QUAD // HEAD), axis=0) * spread

    def collapse(product, spread):
        picked = product * spread
        total = picked[: d.lat]
        for h in range(1, QUAD // HEAD):
            total = total + picked[h * d.lat : (h + 1) * d.lat]
        return total

    groups = [slice(g * d.lat, (g + 1) * d.lat) for g in range(d.groups)]

    def head_mean(values, ones):
        return group_sum(values, ones) * (1.0 / HEAD)

    loads[2].wait()

    def columns(n, part):
        return pl.ds(part * width + n * QUAD, QUAD)

    def key_columns(n):
        return pl.ds(n * d.keys, d.keys)

    def forward_quad(n):
        ones = ones_e()
        spread = same((d.keys, QUAD), d.lat, HEAD).astype(bf16)
        normed = normed_s[...]
        cast = []
        for part in range(2):
            raw = dot(normed, wq_v[:, columns(n, part)])
            fac = lax.rsqrt(head_mean(raw * raw, ones) + epsilon)
            raw_s[:, columns(n, part)] = raw
            fac_s[:, columns(n, part)] = fac
            cast.append((raw * fac).astype(bf16))
            qkv_s[:, columns(n, part)] = cast[part]
        value = dot(normed, wq_v[:, columns(n, 2)]).astype(bf16)
        qkv_s[:, columns(n, 2)] = value
        query, key = cast
        scores = jnp.concatenate(
            [dot_nt(query[g], expand(key[g], spread)) for g in groups], axis=0
        )
        exp_scores = jnp.exp(scores * score_scale) * maskf[...]
        attn = exp_scores / group_sum(exp_scores, ones_k())
        attn_s[:, key_columns(n)] = attn
        attn_b = attn.astype(bf16)
        attended = jnp.concatenate(
            [dot(attn_b[g], expand(value[g], spread)) for g in groups], axis=0
        )
        att_s[:, columns(n, 0)] = attended.astype(bf16)

    for n in range(d.quads):
        if n == d.quads - 1:
            gather_pair(flow_full, recv_f, 3, 12)
        forward_quad(n)

    att_s[...] = dot(permutation(d, block_to_group, False), att_s[...]).astype(bf16)
    loads[3].wait()
    lev_copy(recv_fp, recv_fp, 12, partner).wait_recv()
    flow_a[...] = load_pieces(flow_full).astype(bf16)

    z_at = me >> log2(d.nx)
    x_at = me & (d.nx - 1)
    x_next, x_prev = (x_at + 1) & (d.nx - 1), (x_at - 1) & (d.nx - 1)
    x_far = (x_at + 2) & (d.nx - 1)
    half_rows = d.out_rows // 2
    top, bottom = pl.ds(0, half_rows), pl.ds(half_rows, half_rows)
    sides = ((x_next, top, 0), (x_prev, bottom, 1))
    reach = d.nz // 2
    order = [reach] + [o for k in range(reach - 1, 0, -1) for o in (k, -k)] + [0]
    z_next, z_prev = (z_at + 1) & (d.nz - 1), (z_at - 1) & (d.nz - 1)
    x_sems = 15
    z_sems = x_sems + 4 * d.chunks

    def apart(offset):
        return (z_at + offset) & (d.nz - 1)

    def chunk_blocks(step):
        return [(n, apart(order[step * d.per + n])) for n in range(d.per)]

    def column(x):
        return z_at * d.nx + x

    def far_copy(src, dst, x_to, step, side):
        return lat_copy(src, dst, 5, column(x_to), x_sems + side * d.chunks + step)

    def near_copy(src, dst, x_to, step, side):
        return lat_copy(src, dst, 9, column(x_to), x_sems + (2 + side) * d.chunks + step)

    def mix_chunk(step):
        for n, z in chunk_blocks(step):
            cols = d.nx * d.out_rows
            start = pl.multiple_of(z * cols, cols)
            part = dot_tn(att_s[:, pl.ds(start, cols)], flow_a[...]) * d.grad_scale
            mg_s[z] = part.reshape(d.nx, d.out_rows, width).astype(bf16)
        for x_to, rows, side in sides:
            for n, z in chunk_blocks(step):
                far_copy(
                    mg_s.at[z, x_far, rows], recv_ga.at[side, step, n], x_to, step, side
                ).start()

    def relay_chunk(step):
        for x_to, rows, side in sides:
            arrived = recv_ga.at[side, step]
            far_copy(arrived, arrived, x_to, step, side).wait_recv()
            for n, z in chunk_blocks(step):
                mine = mg_s[z, x_to, rows].astype(f32) + recv_ga[side, step, n].astype(f32)
                mg_s[z, x_to, rows] = mine.astype(bf16)
                near_copy(
                    mg_s.at[z, x_to], recv_gb.at[side, step, n], x_to, step, side
                ).start()

    def ring_copy(src, dst, side, step):
        z_to = z_next if side == 0 else z_prev
        send = 15 if step == 0 else 10
        return lat_copy(src, dst, send, z_to * d.nx + x_at, z_sems + side * reach + step)

    def ring_arrival(side, step):
        slot = recv_g2.at[side, step, top] if step == 0 else recv_g2.at[side, step]
        ring_copy(slot, slot, side, step).wait_recv()
        if step == 0:
            return (top if side == 0 else bottom), recv_g2[side, step, top].astype(f32)
        return pl.ds(0, d.out_rows), recv_g2[side, step].astype(f32)

    def ring_step(step):
        for side in range(2):
            z = apart((reach - step) * (1 if side == 0 else -1))
            if step == 0:
                rows = top if side == 0 else bottom
                ring_copy(send_g2.at[z, rows], recv_g2.at[side, 0, top], side, 0).start()
                continue
            rows, value = ring_arrival(side, step - 1)
            send_g2[z, rows] = (send_g2[z, rows].astype(f32) + value).astype(bf16)
            ring_copy(send_g2.at[z], recv_g2.at[side, step], side, step).start()

    def finish_chunk(step):
        for x_to, rows, side in sides:
            arrived = recv_gb.at[side, step]
            near_copy(arrived, arrived, x_to, step, side).wait_recv()
        for n, z in chunk_blocks(step):
            total = mg_s[z, x_at].astype(f32)
            for side in range(2):
                total = total + recv_gb[side, step, n].astype(f32)
            send_g2[z] = total.astype(bf16)
        if step < reach:
            ring_step(step)

    for step in range(d.chunks):
        mix_chunk(step)

    flow_g[...] = dot(permutation(d, block_to_group, True), flow_a[...]).astype(bf16)

    def backward_quad(n):
        ones = ones_e()
        spread = same((d.keys, QUAD), d.lat, HEAD)
        spread_b = spread.astype(bf16)
        rows = columns(n, 0)
        d_att = dot_nt(flow_g[...], wm_v[rows, :]).astype(bf16)
        query = qkv_s[:, columns(n, 0)]
        key = qkv_s[:, columns(n, 1)]
        value = qkv_s[:, columns(n, 2)]
        attn = attn_s[:, key_columns(n)]
        attn_b = attn.astype(bf16)
        d_attn = jnp.concatenate(
            [dot_nt(d_att[g], expand(value[g], spread_b)) for g in groups], axis=0
        )
        inner = group_sum(attn * d_attn, ones_k())
        d_scores = (attn * (d_attn - inner) * score_scale).astype(bf16)
        d_value = jnp.concatenate(
            [collapse(dot_tn(attn_b[g], d_att[g]), spread) for g in groups], axis=0
        )
        d_key = jnp.concatenate(
            [collapse(dot_tn(d_scores[g], query[g]), spread) for g in groups], axis=0
        )
        d_query = jnp.concatenate(
            [dot(d_scores[g], expand(key[g], spread_b)) for g in groups], axis=0
        )
        gp_s[:, columns(n, 2)] = d_value.astype(bf16)
        for part, upstream in ((0, d_query), (1, d_key)):
            up = upstream.astype(bf16).astype(f32)
            raw = raw_s[:, columns(n, part)]
            fac = fac_s[:, columns(n, part)]
            mean = head_mean(up * raw, ones)
            gp_s[:, columns(n, part)] = (fac * up - raw * (fac * fac * fac) * mean).astype(bf16)

    def project_back(n):
        cols = columns(n, 0)
        dn_s[:, cols] = dot_nt(gp_s[...], wq_v[cols, :])

    def return_group(group):
        far = reach - group
        for offset in (far, 0 if group == 0 else -far):
            z = apart(offset)
            for k in range(offset == 0, d.nx):
                peer = z * d.nx + ((x_at + k) & (d.nx - 1))
                lat_copy(send_d.at[peer], recv_d.at[me], 8, peer).start()

    for n in range(d.quads):
        backward_quad(n)
        relay_chunk(n)
        if n == 0:
            store_pieces(send_m, dot(att_s[...], wm_v[...]))
            scatter_pair(send_m, recv_mp, 4)
        if n == 1:
            scatter_ring(send_m, recv_mp, 4, sum_m, recv_m, 13)

    for n in range(d.quads):
        project_back(n)
        if n == d.quads - 1:
            finish_chunk(0)

    x_group = xg[...].astype(f32)
    d_normed = dn_s[...]
    factor = rx_s[:, :1]
    mean = jnp.mean(d_normed * x_group, axis=-1, keepdims=True)
    d_group = (factor * d_normed - x_group * (factor * factor * factor * mean)).astype(bf16)
    send_d[...] = blocks(dot(permutation(d, block_to_group, False), d_group))
    send_ma[...] = level_sum(sum_m, recv_m, 13).astype(bf16)
    all_to_all(send_ma, recv_ma, 6)
    recv_d[me] = send_d[me]
    return_group(0)

    for step in range(1, d.chunks):
        finish_chunk(step)
        if step < reach:
            return_group(step)
        if step == 2:
            all_to_all_done(send_ma, recv_ma, 6).wait_recv()
            gather_ring(recv_ma, mix_full, 7)
    gather_pair(mix_full, recv_m, 7, 14)

    to_lat = permutation(d, lat_to_block, False)
    lev_copy(recv_mp, recv_mp, 14, partner).wait_recv()
    mixed = (flat(send_t) + scale_ref[...] * load_pieces(mix_full)).astype(bf16)
    out_ref[...] = dot(to_lat, mixed).astype(bf16)

    all_to_all_done(send_d, recv_d, 8).wait_recv()
    d_lat = dot(to_lat, flat(recv_d).astype(bf16))
    dtok_ref[...] = (cot_v[...].astype(f32) + d_lat).astype(bf16)

    mg_ref[...] = send_g2[z_at].astype(f32)
    for side in range(2):
        rows, value = ring_arrival(side, reach - 1)
        mg_ref[rows, :] = mg_ref[rows, :] + value

    for send, recv, sem in (
        (send_t, recv_t, 0),
        (send_fa, recv_fa, 2),
        (send_ma, recv_ma, 6),
        (send_d, recv_d, 8),
    ):
        all_to_all_done(send, recv, sem).wait_send()
    for pair_ref, ring_ref, sems in (
        (recv_fp, recv_f, (1, 11, 3, 12)),
        (recv_mp, recv_m, (4, 13, 7, 14)),
    ):
        for sem, ref in zip(sems, (pair_ref, ring_ref, ring_ref, pair_ref)):
            lev_copy(ref, ref, sem, partner).wait_send()
    sent = [(recv_ga, 5), (recv_gb, 9), (recv_g2.at[:, 0, top], 15)]
    if reach > 1:
        sent.append((recv_g2.at[:, pl.ds(1, reach - 1)], 10))
    for ref, sem in sent:
        lat_copy(ref, ref, sem, column(x_next), x_sems).wait_send()


def hand_over(*refs):
    for src, dst in zip(refs[:3], refs[3:]):
        dst[...] = src[...]


def on_device(x_chips, tokens, key_mask, w_qkv, w_mix, level_scale, cotangent):
    batch, _, band_rows, lon, width = tokens.shape
    nl, nv = lax.axis_size("lat"), lax.axis_size("lev")
    d = SimpleNamespace(
        nl=nl, nv=nv, batch=batch, rb=band_rows, lon=lon, width=width, pl=lon // nl,
        lat=nl * band_rows, tokens=batch * band_rows * lon, piece=width // nv,
        nx=x_chips, nz=nl // x_chips, quads=width // QUAD, out_rows=width // nl,
    )
    d.m = d.tokens // nl
    d.groups = batch * d.pl
    d.keys = (QUAD // HEAD) * d.lat
    d.per = QUAD // (d.nx * d.out_rows)
    d.chunks = d.nz // d.per
    d.grad_scale = 1.0 / math.sqrt(batch * d.lat * lon)
    flat_shape = (d.tokens, width)
    block = (nl, d.m, width)
    part = (nl, d.m, d.piece)
    half = (nv // 2,) + part
    parts = (nv // 2 - 1,) + part
    whole = (nv,) + part

    def vmem(shape, dtype=bf16):
        return pltpu.VMEM(shape, dtype)

    scratch = [
        vmem(flat_shape),
        vmem(flat_shape),
        vmem((width, 3 * width)),
        vmem((width, width)),
        vmem(block),
        vmem(block),
        vmem(whole),
        vmem(half),
        vmem(half),
        vmem(parts),
        vmem(part),
        vmem(part),
        vmem(whole),
        vmem(whole),
        vmem(half),
        vmem(half),
        vmem(parts),
        vmem(part),
        vmem(part),
        vmem(whole),
        vmem(block),
        vmem(block),
        vmem((d.nz, d.nx, d.out_rows, width)),
        vmem((2, d.chunks, d.per, d.out_rows // 2, width)),
        vmem((2, d.chunks, d.per, d.out_rows, width)),
        vmem((d.nz, d.out_rows, width)),
        vmem((2, d.nz // 2, d.out_rows, width)),
        vmem(flat_shape),
        vmem((d.tokens, 128), f32),
        vmem(flat_shape),
        vmem((d.tokens, 2 * width), f32),
        vmem((d.tokens, 2 * width), f32),
        vmem((d.tokens, 3 * width)),
        vmem((d.tokens, d.quads * d.keys), f32),
        vmem(flat_shape),
        vmem(flat_shape),
        vmem(flat_shape),
        vmem((d.tokens, 3 * width)),
        vmem(flat_shape, f32),
        vmem((d.tokens, d.keys), f32),
        pltpu.SemaphoreType.DMA((4,)),
        pltpu.SemaphoreType.DMA((16,)),
        pltpu.SemaphoreType.DMA((15 + 4 * d.chunks + d.nz,)),
    ]
    any_space = pl.BlockSpec(memory_space=pl.ANY)
    in_vmem = pl.BlockSpec(memory_space=pltpu.VMEM)
    results = pl.pallas_call(
        functools.partial(kernel, d),
        name="latitude_block",
        out_shape=(
            jax.ShapeDtypeStruct(flat_shape, bf16),
            jax.ShapeDtypeStruct(flat_shape, bf16),
            jax.ShapeDtypeStruct((d.out_rows, width), f32),
        ),
        in_specs=[any_space, in_vmem, any_space, any_space, in_vmem, any_space],
        out_specs=(in_vmem, in_vmem, in_vmem),
        scratch_shapes=scratch,
        compiler_params=pltpu.CompilerParams(
            collective_id=0, has_side_effects=True, vmem_limit_bytes=60 * 1024 * 1024
        ),
    )(
        tokens.reshape(flat_shape),
        key_mask,
        w_qkv,
        w_mix.reshape(width, width),
        level_scale,
        cotangent.reshape(flat_shape),
    )
    output, d_tokens, mix_grad = pl.pallas_call(
        hand_over,
        name="hand_over",
        out_shape=tuple(jax.ShapeDtypeStruct(x.shape, x.dtype) for x in results),
        in_specs=[in_vmem] * 3,
        out_specs=(in_vmem,) * 3,
    )(*results)
    return (
        output.reshape(tokens.shape),
        d_tokens.reshape(tokens.shape),
        mix_grad.reshape(1, d.out_rows, width),
    )


def solution(mesh, x_chips=X_CHIPS):
    return jax.shard_map(
        functools.partial(on_device, x_chips),
        mesh=mesh,
        in_specs=(
            P(None, "lev", "lat", None, None),
            P(),
            P(),
            P("lev", None, None),
            P("lev", None),
            P(None, "lev", "lat", None, None),
        ),
        out_specs=(
            P(None, "lev", "lat", None, None),
            P(None, "lev", "lat", None, None),
            P("lev", "lat", None),
        ),
        check_vma=False,
    )
```

```python
import functools
import math
from types import SimpleNamespace

import jax
import jax.numpy as jnp
from jax import lax
from jax.experimental import pallas as pl
from jax.experimental.pallas import tpu as pltpu
from jax.sharding import PartitionSpec as P

HEAD = 64
QUAD = 256
X_CHIPS = 4
epsilon = 1e-06
score_scale = 0.25
f32 = jnp.float32
bf16 = jnp.bfloat16
MESH = pl.DeviceIdType.MESH


def dot(a, b):
    return lax.dot_general(a, b, (((1,), (0,)), ((), ())), preferred_element_type=f32)


def dot_nt(a, b):
    return lax.dot_general(a, b, (((1,), (1,)), ((), ())), preferred_element_type=f32)


def dot_tn(a, b):
    return lax.dot_general(a, b, (((0,), (0,)), ((), ())), preferred_element_type=f32)


def log2(n):
    return n.bit_length() - 1


def lat_to_block(d, a):
    j = a >> log2(d.m)
    b = (a >> log2(d.rb * d.pl)) & (d.batch - 1)
    r = (a >> log2(d.pl)) & (d.rb - 1)
    p = a & (d.pl - 1)
    return (b * d.rb + r) * d.lon + j * d.pl + p


def block_to_group(d, c):
    b = c >> log2(d.pl * d.lat)
    p = (c >> log2(d.lat)) & (d.pl - 1)
    i = (c & (d.lat - 1)) >> log2(d.rb)
    r = c & (d.rb - 1)
    return i * d.m + b * d.rb * d.pl + r * d.pl + p


def permutation(d, index, forward):
    rows = lax.broadcasted_iota(jnp.int32, (d.tokens, d.tokens), 0)
    cols = lax.broadcasted_iota(jnp.int32, (d.tokens, d.tokens), 1)
    hit = index(d, rows) == cols if forward else index(d, cols) == rows
    return jnp.where(hit, 1.0, 0.0).astype(bf16)


def group_sum(values, ones):
    return dot(values.astype(bf16), ones)


def kernel(
    d,
    tok_hbm,
    mask_ref,
    wq_hbm,
    wm_hbm,
    scale_ref,
    cot_hbm,
    out_ref,
    dtok_ref,
    mg_ref,
    tok_v,
    cot_v,
    wq_v,
    wm_v,
    send_t,
    recv_t,
    send_f,
    recv_fp,
    sum_f,
    recv_f,
    send_fa,
    recv_fa,
    flow_full,
    send_m,
    recv_mp,
    sum_m,
    recv_m,
    send_ma,
    recv_ma,
    mix_full,
    send_d,
    recv_d,
    mg_s,
    recv_ga,
    recv_gb,
    send_g2,
    recv_g2,
    xg,
    rx_s,
    normed_s,
    raw_s,
    fac_s,
    qkv_s,
    attn_s,
    att_s,
    flow_g,
    gp_s,
    dn_s,
    maskf,
    load_sem,
    send_sem,
    recv_sem,
):
    me = lax.axis_index("lat")
    lv = lax.axis_index("lev")
    nl, nv, m, width, tokens = d.nl, d.nv, d.m, d.width, d.tokens
    ny = nv // 2
    piece = d.piece
    loads = [
        pltpu.make_async_copy(src, dst, load_sem.at[n])
        for n, (src, dst) in enumerate(
            ((tok_hbm, tok_v), (cot_hbm, cot_v), (wq_hbm, wq_v), (wm_hbm, wm_v))
        )
    ]
    for load in loads:
        load.start()

    barrier = pltpu.get_barrier_semaphore()

    def greet_lat(k, carry):
        pl.semaphore_signal(
            barrier, inc=1, device_id={"lat": lax.rem(me + k, nl)}, device_id_type=MESH
        )
        return carry

    lax.fori_loop(1, nl, greet_lat, 0)
    pl.semaphore_signal(barrier, inc=1, device_id={"lev": lv ^ 1}, device_id_type=MESH)
    for k in range(1, ny):
        y_to = ((lv >> 1) + k) & (ny - 1)
        pl.semaphore_signal(
            barrier, inc=1, device_id={"lev": y_to * 2 + (lv & 1)}, device_id_type=MESH
        )

    def lat_copy(src, dst, sem, peer, recv=None):
        return pltpu.make_async_remote_copy(
            src_ref=src,
            dst_ref=dst,
            send_sem=send_sem.at[sem],
            recv_sem=recv_sem.at[sem if recv is None else recv],
            device_id={"lat": peer},
            device_id_type=MESH,
        )

    def lev_copy(src, dst, sem, peer):
        return pltpu.make_async_remote_copy(
            src_ref=src,
            dst_ref=dst,
            send_sem=send_sem.at[sem],
            recv_sem=recv_sem.at[sem],
            device_id={"lev": peer},
            device_id_type=MESH,
        )

    def all_to_all(send, recv, sem):
        def body(k, carry):
            peer = lax.rem(me + k, nl)
            lat_copy(send.at[peer], recv.at[me], sem, peer).start()
            return carry

        lax.fori_loop(1, nl, body, 0)
        recv[me] = send[me]

    def all_to_all_done(send, recv, sem):
        return lat_copy(
            send.at[pl.ds(0, nl - 1)], recv.at[pl.ds(0, nl - 1)], sem, lax.rem(me + 1, nl)
        )

    y_at, core = lv >> 1, lv & 1
    partner = lv ^ 1
    own_piece = core * ny + y_at
    mine, other = pl.ds(core * ny, ny), pl.ds((1 - core) * ny, ny)
    next_y = ((y_at + 1) & (ny - 1)) * 2 + core

    def scatter_pair(send, recv_p, sem):
        lev_copy(send.at[other], recv_p, sem, partner).start()

    def scatter_ring(send, recv_p, pair_sem, part_sum, recv, sem):
        lev_copy(recv_p, recv_p, pair_sem, partner).wait_recv()
        part_sum[...] = (send[mine].astype(f32) + recv_p[...].astype(f32)).astype(bf16)
        for k in range(1, ny):
            y_to = (y_at + k) & (ny - 1)
            lev_copy(part_sum.at[y_to], recv.at[k - 1], sem, y_to * 2 + core).start()

    def level_sum(part_sum, recv, sem):
        lev_copy(recv, recv, sem, next_y).wait_recv()
        total = part_sum[y_at].astype(f32)
        for k in range(ny - 1):
            total = total + recv[k].astype(f32)
        return total

    def gather_ring(block, full, sem):
        for k in range(1, ny):
            y_to = (y_at + k) & (ny - 1)
            lev_copy(block, full.at[own_piece], sem, y_to * 2 + core).start()
        full[own_piece] = block[...]

    def gather_pair(full, recv, ring_sem, sem):
        lev_copy(recv, recv, ring_sem, next_y).wait_recv()
        lev_copy(full.at[mine], full.at[mine], sem, partner).start()

    def flat(ref):
        return ref[...].astype(f32).reshape(tokens, width)

    def blocks(values):
        return values.reshape(nl, m, width).astype(bf16)

    def store_pieces(ref, values):
        for q in range(nv):
            part = values[:, q * piece : (q + 1) * piece]
            ref[q] = part.reshape(nl, m, piece).astype(bf16)

    def load_pieces(ref):
        parts = [ref[q].astype(f32).reshape(tokens, piece) for q in range(nv)]
        return jnp.concatenate(parts, axis=1)

    to_block = permutation(d, lat_to_block, True)
    loads[0].wait()
    send_t[...] = blocks(dot(to_block, tok_v[...]))
    loads[1].wait()
    store_pieces(send_f, scale_ref[...] * dot(to_block, cot_v[...]))

    pl.semaphore_wait(barrier, nl - 1 + ny)
    scatter_pair(send_f, recv_fp, 1)
    z_here, x_here = me >> log2(d.nx), me & (d.nx - 1)
    far_first = [d.nz // 2] + [o for k in range(d.nz // 2 - 1, 0, -1) for o in (k, -k)] + [0]
    for offset in far_first:
        for k in range(offset == 0, d.nx):
            peer = ((z_here + offset) & (d.nz - 1)) * d.nx + ((x_here + k) & (d.nx - 1))
            lat_copy(send_t.at[peer], recv_t.at[me], 0, peer).start()
    recv_t[me] = send_t[me]

    valid = mask_ref[...].astype(f32)
    for b in range(d.batch):
        row = jnp.concatenate([valid[b : b + 1]] * (QUAD // HEAD), axis=1)
        maskf[pl.ds(b * d.pl * d.lat, d.pl * d.lat), :] = jnp.broadcast_to(
            row, (d.pl * d.lat, d.keys)
        )

    scatter_ring(send_f, recv_fp, 1, sum_f, recv_f, 11)
    send_fa[...] = level_sum(sum_f, recv_f, 11).astype(bf16)
    all_to_all(send_fa, recv_fa, 2)

    all_to_all_done(send_t, recv_t, 0).wait_recv()
    x_group = dot(permutation(d, block_to_group, True), flat(recv_t).astype(bf16))
    xg[...] = x_group.astype(bf16)
    factor = lax.rsqrt(jnp.mean(x_group * x_group, axis=-1, keepdims=True) + epsilon)
    rx_s[...] = jnp.broadcast_to(factor, rx_s.shape)
    normed_s[...] = (x_group * factor).astype(bf16)

    all_to_all_done(send_fa, recv_fa, 2).wait_recv()
    gather_ring(recv_fa, flow_full, 3)

    def same(shape, row_size, col_size):
        rows = lax.broadcasted_iota(jnp.int32, shape, 0) >> log2(row_size)
        cols = lax.broadcasted_iota(jnp.int32, shape, 1) >> log2(col_size)
        return jnp.where(rows == cols, 1.0, 0.0)

    def ones_e():
        return same((QUAD, QUAD), HEAD, HEAD).astype(bf16)

    def ones_k():
        return same((d.keys, d.keys), d.lat, d.lat).astype(bf16)

    def expand(block, spread):
        return jnp.concatenate([block] * (QUAD // HEAD), axis=0) * spread

    def collapse(product, spread):
        picked = product * spread
        total = picked[: d.lat]
        for h in range(1, QUAD // HEAD):
            total = total + picked[h * d.lat : (h + 1) * d.lat]
        return total

    groups = [slice(g * d.lat, (g + 1) * d.lat) for g in range(d.groups)]

    def head_mean(values, ones):
        return group_sum(values, ones) * (1.0 / HEAD)

    loads[2].wait()

    def columns(n, part):
        return pl.ds(part * width + n * QUAD, QUAD)

    def key_columns(n):
        return pl.ds(n * d.keys, d.keys)

    def forward_quad(n):
        ones = ones_e()
        spread = same((d.keys, QUAD), d.lat, HEAD).astype(bf16)
        normed = normed_s[...]
        cast = []
        for part in range(2):
            raw = dot(normed, wq_v[:, columns(n, part)])
            fac = lax.rsqrt(head_mean(raw * raw, ones) + epsilon)
            raw_s[:, columns(n, part)] = raw
            fac_s[:, columns(n, part)] = fac
            cast.append((raw * fac).astype(bf16))
            qkv_s[:, columns(n, part)] = cast[part]
        value = dot(normed, wq_v[:, columns(n, 2)]).astype(bf16)
        qkv_s[:, columns(n, 2)] = value
        query, key = cast
        scores = jnp.concatenate(
            [dot_nt(query[g], expand(key[g], spread)) for g in groups], axis=0
        )
        exp_scores = jnp.exp(scores * score_scale) * maskf[...]
        attn = exp_scores / group_sum(exp_scores, ones_k())
        attn_s[:, key_columns(n)] = attn
        attn_b = attn.astype(bf16)
        attended = jnp.concatenate(
            [dot(attn_b[g], expand(value[g], spread)) for g in groups], axis=0
        )
        att_s[:, columns(n, 0)] = attended.astype(bf16)

    for n in range(d.quads):
        if n == d.quads - 1:
            gather_pair(flow_full, recv_f, 3, 12)
        forward_quad(n)

    loads[3].wait()
    lev_copy(recv_fp, recv_fp, 12, partner).wait_recv()
    flow_block = load_pieces(flow_full).astype(bf16)
    flow_g[...] = dot(permutation(d, block_to_group, True), flow_block).astype(bf16)

    z_at = me >> log2(d.nx)
    x_at = me & (d.nx - 1)
    x_next, x_prev = (x_at + 1) & (d.nx - 1), (x_at - 1) & (d.nx - 1)
    x_far = (x_at + 2) & (d.nx - 1)
    half_rows = d.out_rows // 2
    top, bottom = pl.ds(0, half_rows), pl.ds(half_rows, half_rows)
    sides = ((x_next, top, 0), (x_prev, bottom, 1))
    reach = d.nz // 2
    order = [reach] + [o for k in range(reach - 1, 0, -1) for o in (k, -k)] + [0]
    z_next, z_prev = (z_at + 1) & (d.nz - 1), (z_at - 1) & (d.nz - 1)
    x_sems = 15
    z_sems = x_sems + 4 * d.chunks

    def apart(offset):
        return (z_at + offset) & (d.nz - 1)

    def chunk_blocks(step):
        return [(n, apart(order[step * d.per + n])) for n in range(d.per)]

    def column(x):
        return z_at * d.nx + x

    def far_copy(src, dst, x_to, step, side):
        return lat_copy(src, dst, 5, column(x_to), x_sems + side * d.chunks + step)

    def near_copy(src, dst, x_to, step, side):
        return lat_copy(src, dst, 9, column(x_to), x_sems + (2 + side) * d.chunks + step)

    def mix_chunk(step):
        for n, z in chunk_blocks(step):
            cols = d.nx * d.out_rows
            start = pl.multiple_of(z * cols, cols)
            part = dot_tn(att_s[:, pl.ds(start, cols)], flow_g[...]) * d.grad_scale
            mg_s[z] = part.reshape(d.nx, d.out_rows, width).astype(bf16)
        for x_to, rows, side in sides:
            for n, z in chunk_blocks(step):
                far_copy(
                    mg_s.at[z, x_far, rows], recv_ga.at[side, step, n], x_to, step, side
                ).start()

    def relay_chunk(step):
        for x_to, rows, side in sides:
            arrived = recv_ga.at[side, step]
            far_copy(arrived, arrived, x_to, step, side).wait_recv()
            for n, z in chunk_blocks(step):
                mine = mg_s[z, x_to, rows].astype(f32) + recv_ga[side, step, n].astype(f32)
                mg_s[z, x_to, rows] = mine.astype(bf16)
                near_copy(
                    mg_s.at[z, x_to], recv_gb.at[side, step, n], x_to, step, side
                ).start()

    def ring_copy(src, dst, side, step):
        z_to = z_next if side == 0 else z_prev
        send = 15 if step == 0 else 10
        return lat_copy(src, dst, send, z_to * d.nx + x_at, z_sems + side * reach + step)

    def ring_arrival(side, step):
        slot = recv_g2.at[side, step, top] if step == 0 else recv_g2.at[side, step]
        ring_copy(slot, slot, side, step).wait_recv()
        if step == 0:
            return (top if side == 0 else bottom), recv_g2[side, step, top].astype(f32)
        return pl.ds(0, d.out_rows), recv_g2[side, step].astype(f32)

    def ring_step(step):
        for side in range(2):
            z = apart((reach - step) * (1 if side == 0 else -1))
            if step == 0:
                rows = top if side == 0 else bottom
                ring_copy(send_g2.at[z, rows], recv_g2.at[side, 0, top], side, 0).start()
                continue
            rows, value = ring_arrival(side, step - 1)
            send_g2[z, rows] = (send_g2[z, rows].astype(f32) + value).astype(bf16)
            ring_copy(send_g2.at[z], recv_g2.at[side, step], side, step).start()

    def finish_chunk(step):
        for x_to, rows, side in sides:
            arrived = recv_gb.at[side, step]
            near_copy(arrived, arrived, x_to, step, side).wait_recv()
        for n, z in chunk_blocks(step):
            total = mg_s[z, x_at].astype(f32)
            for side in range(2):
                total = total + recv_gb[side, step, n].astype(f32)
            send_g2[z] = total.astype(bf16)
        if step < reach:
            ring_step(step)

    for step in range(d.chunks):
        mix_chunk(step)


    def backward_quad(n):
        ones = ones_e()
        spread = same((d.keys, QUAD), d.lat, HEAD)
        spread_b = spread.astype(bf16)
        rows = columns(n, 0)
        d_att = dot_nt(flow_g[...], wm_v[rows, :]).astype(bf16)
        query = qkv_s[:, columns(n, 0)]
        key = qkv_s[:, columns(n, 1)]
        value = qkv_s[:, columns(n, 2)]
        attn = attn_s[:, key_columns(n)]
        attn_b = attn.astype(bf16)
        d_attn = jnp.concatenate(
            [dot_nt(d_att[g], expand(value[g], spread_b)) for g in groups], axis=0
        )
        inner = group_sum(attn * d_attn, ones_k())
        d_scores = (attn * (d_attn - inner) * score_scale).astype(bf16)
        d_value = jnp.concatenate(
            [collapse(dot_tn(attn_b[g], d_att[g]), spread) for g in groups], axis=0
        )
        d_key = jnp.concatenate(
            [collapse(dot_tn(d_scores[g], query[g]), spread) for g in groups], axis=0
        )
        d_query = jnp.concatenate(
            [dot(d_scores[g], expand(key[g], spread_b)) for g in groups], axis=0
        )
        gp_s[:, columns(n, 2)] = d_value.astype(bf16)
        for part, upstream in ((0, d_query), (1, d_key)):
            up = upstream.astype(bf16).astype(f32)
            raw = raw_s[:, columns(n, part)]
            fac = fac_s[:, columns(n, part)]
            mean = head_mean(up * raw, ones)
            gp_s[:, columns(n, part)] = (fac * up - raw * (fac * fac * fac) * mean).astype(bf16)

    def project_back(n):
        cols = columns(n, 0)
        dn_s[:, cols] = dot_nt(gp_s[...], wq_v[cols, :])

    def return_group(group):
        far = reach - group
        for offset in (far, 0 if group == 0 else -far):
            z = apart(offset)
            for k in range(offset == 0, d.nx):
                peer = z * d.nx + ((x_at + k) & (d.nx - 1))
                lat_copy(send_d.at[peer], recv_d.at[me], 8, peer).start()

    for n in range(d.quads):
        backward_quad(n)
        relay_chunk(n)
        if n == 0:
            att_block = dot(permutation(d, block_to_group, False), att_s[...])
            store_pieces(send_m, dot(att_block.astype(bf16), wm_v[...]))
            scatter_pair(send_m, recv_mp, 4)
        if n == 1:
            scatter_ring(send_m, recv_mp, 4, sum_m, recv_m, 13)

    for n in range(d.quads):
        project_back(n)
        if n == d.quads - 1:
            finish_chunk(0)

    x_group = xg[...].astype(f32)
    d_normed = dn_s[...]
    factor = rx_s[:, :1]
    mean = jnp.mean(d_normed * x_group, axis=-1, keepdims=True)
    d_group = (factor * d_normed - x_group * (factor * factor * factor * mean)).astype(bf16)
    send_d[...] = blocks(dot(permutation(d, block_to_group, False), d_group))
    send_ma[...] = level_sum(sum_m, recv_m, 13).astype(bf16)
    all_to_all(send_ma, recv_ma, 6)
    recv_d[me] = send_d[me]
    return_group(0)

    for step in range(1, d.chunks):
        if step < reach:
            return_group(step)
        finish_chunk(step)
        if step == 2:
            all_to_all_done(send_ma, recv_ma, 6).wait_recv()
            gather_ring(recv_ma, mix_full, 7)
    gather_pair(mix_full, recv_m, 7, 14)

    to_lat = permutation(d, lat_to_block, False)
    lev_copy(recv_mp, recv_mp, 14, partner).wait_recv()
    mixed = (flat(send_t) + scale_ref[...] * load_pieces(mix_full)).astype(bf16)
    out_ref[...] = dot(to_lat, mixed).astype(bf16)

    all_to_all_done(send_d, recv_d, 8).wait_recv()
    d_lat = dot(to_lat, flat(recv_d).astype(bf16))
    dtok_ref[...] = (cot_v[...].astype(f32) + d_lat).astype(bf16)

    mg_ref[...] = send_g2[z_at].astype(f32)
    for side in range(2):
        rows, value = ring_arrival(side, reach - 1)
        mg_ref[rows, :] = mg_ref[rows, :] + value

    for send, recv, sem in (
        (send_t, recv_t, 0),
        (send_fa, recv_fa, 2),
        (send_ma, recv_ma, 6),
        (send_d, recv_d, 8),
    ):
        all_to_all_done(send, recv, sem).wait_send()
    for pair_ref, ring_ref, sems in (
        (recv_fp, recv_f, (1, 11, 3, 12)),
        (recv_mp, recv_m, (4, 13, 7, 14)),
    ):
        for sem, ref in zip(sems, (pair_ref, ring_ref, ring_ref, pair_ref)):
            lev_copy(ref, ref, sem, partner).wait_send()
    sent = [(recv_ga, 5), (recv_gb, 9), (recv_g2.at[:, 0, top], 15)]
    if reach > 1:
        sent.append((recv_g2.at[:, pl.ds(1, reach - 1)], 10))
    for ref, sem in sent:
        lat_copy(ref, ref, sem, column(x_next), x_sems).wait_send()


def hand_over(*refs):
    for src, dst in zip(refs[:3], refs[3:]):
        dst[...] = src[...]


def on_device(x_chips, tokens, key_mask, w_qkv, w_mix, level_scale, cotangent):
    batch, _, band_rows, lon, width = tokens.shape
    nl, nv = lax.axis_size("lat"), lax.axis_size("lev")
    d = SimpleNamespace(
        nl=nl, nv=nv, batch=batch, rb=band_rows, lon=lon, width=width, pl=lon // nl,
        lat=nl * band_rows, tokens=batch * band_rows * lon, piece=width // nv,
        nx=x_chips, nz=nl // x_chips, quads=width // QUAD, out_rows=width // nl,
    )
    d.m = d.tokens // nl
    d.groups = batch * d.pl
    d.keys = (QUAD // HEAD) * d.lat
    d.per = QUAD // (d.nx * d.out_rows)
    d.chunks = d.nz // d.per
    d.grad_scale = 1.0 / math.sqrt(batch * d.lat * lon)
    flat_shape = (d.tokens, width)
    block = (nl, d.m, width)
    part = (nl, d.m, d.piece)
    half = (nv // 2,) + part
    parts = (nv // 2 - 1,) + part
    whole = (nv,) + part

    def vmem(shape, dtype=bf16):
        return pltpu.VMEM(shape, dtype)

    scratch = [
        vmem(flat_shape),
        vmem(flat_shape),
        vmem((width, 3 * width)),
        vmem((width, width)),
        vmem(block),
        vmem(block),
        vmem(whole),
        vmem(half),
        vmem(half),
        vmem(parts),
        vmem(part),
        vmem(part),
        vmem(whole),
        vmem(whole),
        vmem(half),
        vmem(half),
        vmem(parts),
        vmem(part),
        vmem(part),
        vmem(whole),
        vmem(block),
        vmem(block),
        vmem((d.nz, d.nx, d.out_rows, width)),
        vmem((2, d.chunks, d.per, d.out_rows // 2, width)),
        vmem((2, d.chunks, d.per, d.out_rows, width)),
        vmem((d.nz, d.out_rows, width)),
        vmem((2, d.nz // 2, d.out_rows, width)),
        vmem(flat_shape),
        vmem((d.tokens, 128), f32),
        vmem(flat_shape),
        vmem((d.tokens, 2 * width), f32),
        vmem((d.tokens, 2 * width), f32),
        vmem((d.tokens, 3 * width)),
        vmem((d.tokens, d.quads * d.keys), f32),
        vmem(flat_shape),
        vmem(flat_shape),
        vmem((d.tokens, 3 * width)),
        vmem(flat_shape, f32),
        vmem((d.tokens, d.keys), f32),
        pltpu.SemaphoreType.DMA((4,)),
        pltpu.SemaphoreType.DMA((16,)),
        pltpu.SemaphoreType.DMA((15 + 4 * d.chunks + d.nz,)),
    ]
    any_space = pl.BlockSpec(memory_space=pl.ANY)
    in_vmem = pl.BlockSpec(memory_space=pltpu.VMEM)
    results = pl.pallas_call(
        functools.partial(kernel, d),
        name="latitude_block",
        out_shape=(
            jax.ShapeDtypeStruct(flat_shape, bf16),
            jax.ShapeDtypeStruct(flat_shape, bf16),
            jax.ShapeDtypeStruct((d.out_rows, width), f32),
        ),
        in_specs=[any_space, in_vmem, any_space, any_space, in_vmem, any_space],
        out_specs=(in_vmem, in_vmem, in_vmem),
        scratch_shapes=scratch,
        compiler_params=pltpu.CompilerParams(
            collective_id=0, has_side_effects=True, vmem_limit_bytes=60 * 1024 * 1024
        ),
    )(
        tokens.reshape(flat_shape),
        key_mask,
        w_qkv,
        w_mix.reshape(width, width),
        level_scale,
        cotangent.reshape(flat_shape),
    )
    output, d_tokens, mix_grad = pl.pallas_call(
        hand_over,
        name="hand_over",
        out_shape=tuple(jax.ShapeDtypeStruct(x.shape, x.dtype) for x in results),
        in_specs=[in_vmem] * 3,
        out_specs=(in_vmem,) * 3,
    )(*results)
    return (
        output.reshape(tokens.shape),
        d_tokens.reshape(tokens.shape),
        mix_grad.reshape(1, d.out_rows, width),
    )


def solution(mesh, x_chips=X_CHIPS):
    return jax.shard_map(
        functools.partial(on_device, x_chips),
        mesh=mesh,
        in_specs=(
            P(None, "lev", "lat", None, None),
            P(),
            P(),
            P("lev", None, None),
            P("lev", None),
            P(None, "lev", "lat", None, None),
        ),
        out_specs=(
            P(None, "lev", "lat", None, None),
            P(None, "lev", "lat", None, None),
            P("lev", "lat", None),
        ),
        check_vma=False,
    )
```
